512 devices in a mesh: pool: 32 (over z, y_hi), band: 16 (over y_lo, x, core).
Axes of the slice: x: 4, y: 4 (y_hi: 2, y_lo: 2; y = y_hi * 2 + y_lo), z: 16, core: 2. Of those that a mesh axis runs over, the one named last changes fastest.
Arguments:
- orbitals: bfloat16 [32, 16, 2, 46656], P('pool', 'band'), may hold values from -6 to 6
- occupation: int32 [32, 16], P('pool', 'band'), may hold values from 1 to 2
- kernel: float32 [46656], replicated, may hold values from 0.02 to 2
Outputs:
- exchanged: bfloat16 [32, 16, 2, 46656], P('pool', 'band')
- gram_matrix: float32 [32, 2, 16, 16], P('pool', None, None, 'band')
The draws below stay inside these ranges and needn't reach their ends.
All inputs are finite; a program needn't handle non-finite values.
Results may differ from the reference program's by a relative error of at most 0.013.
Values may be sent and summed in bfloat16 or wider, within the bound.
A program may use at most 64 MiB of HBM per device.

```python
import math
import jax
import jax.numpy as jnp
from jax import lax

NG = 36
BAND_DEV = 1
GRID = 46656
NB = 16
K = 32
N_POOL = 32
N_BAND = 16


def place_ends(drawn, stream_key, low, largest):
    dims = drawn.shape
    spot = [jax.random.randint(jax.random.fold_in(stream_key, axis), (), 0, dims[axis]) for axis in range(len(dims))]
    drawn = drawn.at[tuple(spot)].set(low)
    longest = dims.index(max(dims))
    spot[longest] = (spot[longest] + 1) % dims[longest]
    return drawn.at[tuple(spot)].set(largest)


def block_scale(rng, shape, cuts, low, high):
    factor_of, own = 1.0, jax.random.fold_in(rng, 6)
    for dim, shards_of in cuts:
        draws = jnp.exp(jax.random.uniform(jax.random.fold_in(own, dim), (shards_of,), jnp.float32, low / len(cuts), high / len(cuts)))
        factor_of = factor_of * jnp.repeat(draws, shape[dim] // shards_of).reshape([-1 if axis == dim else 1 for axis in range(len(shape))])
    return factor_of


def gaussian(rng, extent, scale, most, cuts=(), kind=jnp.bfloat16):
    array = jax.random.normal(rng, extent, jnp.float32) * scale
    if len(cuts) > 0:
        array = block_scale(rng, extent, cuts, -0.22, 0.18) * array
    return jnp.clip(array, min=-most, max=most).astype(kind)


def setup_inputs(seed: int = 0) -> dict:
    keys = jax.random.split(jax.random.key(seed), 4)
    orbitals = gaussian(keys[0], (K, NB, 2, GRID), 1.0, 6.0, ((0, 32), (1, 16)))
    occupation = place_ends(jax.random.randint(keys[1], (K, NB), 1, 3), jax.random.fold_in(keys[1], 1), 1, 2).astype(jnp.int32)
    kernel = jnp.clip(jnp.exp(jax.random.uniform(keys[2], (GRID,), jnp.float32, math.log(0.02), math.log(2.0))), 0.02, 2.0)
    return dict(orbitals=orbitals, occupation=occupation, kernel=kernel)


def start_of(*values):
    return tuple((jnp.asarray(value, dtype=jnp.int32) for value in values))

def dft_matrix(direction):
    points = jnp.arange(NG, dtype=jnp.int32)
    phases = points[:, None] * points[None, :] % NG
    angles = 2.0 * math.pi / NG * phases.astype(jnp.float32)
    cosine = jnp.cos(angles)
    sine = direction * jnp.sin(angles)
    blocks = jnp.stack([jnp.stack([cosine, sine]), jnp.stack([-sine, cosine])])
    return jnp.transpose(blocks, (0, 2, 1, 3)).astype(jnp.bfloat16)

def transform(values, matrix, keep_float):
    count = values.shape[0]
    current = values.reshape(count, 2, NG, NG * NG)
    for axis_pass in range(3):
        product = jnp.einsum('uavb,pvbc->puca', matrix.astype(jnp.float32), current.astype(jnp.float32), precision=lax.Precision.HIGHEST)
        product = product.reshape(count, 2, NG, NG * NG)
        if axis_pass == 2 and keep_float:
            current = product
        else:
            current = product.astype(jnp.bfloat16)
    return current.reshape(count, 2, NG * NG * NG)

def add_block(accum_real, accum_imag, local_bands, visiting, visiting_occ, kernel, forward_matrix, inverse_matrix):
    c = local_bands[:, 0].astype(jnp.float32)
    d = local_bands[:, 1].astype(jnp.float32)
    for j in range(visiting.shape[0]):
        a = visiting[j, 0].astype(jnp.float32)
        b = visiting[j, 1].astype(jnp.float32)
        density = jnp.stack([a * c + b * d, a * d - b * c], axis=1).astype(jnp.bfloat16)
        spectrum = transform(density, forward_matrix, False)
        screened = (spectrum.astype(jnp.float32) * (kernel / GRID)).astype(jnp.bfloat16)
        potential = transform(screened, inverse_matrix, True)
        weight = -0.5 * visiting_occ[j].astype(jnp.float32)
        e = potential[:, 0]
        f = potential[:, 1]
        accum_real = accum_real + weight * (a * e - b * f)
        accum_imag = accum_imag + weight * (a * f + b * e)
    return (accum_real, accum_imag)

def contract(x, y):
    return jnp.einsum('ig,jg->ij', x.astype(jnp.float32), y.astype(jnp.float32), precision=lax.Precision.HIGHEST)

def gram_block(bra_rows, ket_rows):
    c = bra_rows[:, 0]
    d = bra_rows[:, 1]
    e = ket_rows[:, 0]
    f = ket_rows[:, 1]
    real_part = contract(c, e) + contract(d, f)
    imag_part = contract(c, f) - contract(d, e)
    return jnp.stack([real_part, imag_part])

def reference(orbitals, occupation, kernel):
    forward_matrix = dft_matrix(1.0)
    inverse_matrix = dft_matrix(-1.0)

    def per_group(pool_index, group_index):
        before = (pool_index + N_POOL - 1) % N_POOL
        prior = (group_index + N_BAND - 1) % N_BAND
        local_bands = lax.dynamic_slice(orbitals, start_of(pool_index, group_index * BAND_DEV, 0, 0), (1, BAND_DEV, 2, GRID))[0]
        first_block = lax.dynamic_slice(orbitals, start_of(before, group_index * BAND_DEV, 0, 0), (1, BAND_DEV, 2, GRID))[0]
        second_block = lax.dynamic_slice(orbitals, start_of(before, prior * BAND_DEV, 0, 0), (1, BAND_DEV, 2, GRID))[0]
        first_occ = lax.dynamic_slice(occupation, start_of(before, group_index * BAND_DEV), (1, BAND_DEV))[0]
        second_occ = lax.dynamic_slice(occupation, start_of(before, prior * BAND_DEV), (1, BAND_DEV))[0]
        zeros_grid = jnp.zeros((BAND_DEV, GRID), jnp.float32)
        accum_real, accum_imag = add_block(zeros_grid, zeros_grid, local_bands, first_block, first_occ, kernel, forward_matrix, inverse_matrix)
        accum_real, accum_imag = add_block(accum_real, accum_imag, local_bands, second_block, second_occ, kernel, forward_matrix, inverse_matrix)
        return jnp.stack([accum_real, accum_imag], axis=1).astype(jnp.bfloat16)
    groups = jnp.arange(N_BAND, dtype=jnp.int32)

    def per_pool(pool_index):
        return jax.vmap(lambda group_index: per_group(pool_index, group_index))(groups)
    exchanged = lax.map(per_pool, jnp.arange(N_POOL, dtype=jnp.int32)).reshape(N_POOL, BAND_DEV * N_BAND, 2, GRID)
    norm_factor = 1.0 / math.sqrt(GRID)

    def pool_gram(both):
        return gram_block(both[0], both[1]) * norm_factor
    gram_matrix = lax.map(pool_gram, (orbitals, exchanged))
    return (exchanged, gram_matrix)
```

```python
import functools
import math

import jax
import jax.numpy as jnp
import numpy as np
from jax import lax
from jax.experimental import pallas as pl
from jax.experimental.pallas import tpu as pltpu
from jax.sharding import PartitionSpec as P

NG = 36
GRID = 46656
SIDE = 216
NX = 4
F32 = jnp.float32
BF16 = jnp.bfloat16


def tables():
    index = np.arange(SIDE)
    x, y_high = index // 6, index % 6
    rows = (np.outer(x, x) + 6 * np.outer(y_high, y_high)) % NG
    y_low, z = index // NG, index % NG
    lanes = (np.outer(z, z) + 6 * np.outer(y_low, y_low)) % NG
    twiddle = np.outer(y_high, y_low) % NG
    step = 2.0 * math.pi / NG
    mats = np.stack([np.cos(step * rows), np.sin(step * rows), np.cos(step * lanes), np.sin(step * lanes)])
    turns = np.stack([np.cos(step * twiddle), np.sin(step * twiddle)])
    return jnp.asarray(mats.astype(np.float32)).astype(BF16), jnp.asarray(turns.astype(np.float32))


def dot(a, b):
    return jnp.dot(a, b, preferred_element_type=F32)


def exchange_pair(own, other, weight, mats, twiddle, kernel):
    c, d = own[0].astype(F32), own[1].astype(F32)
    a, b = other[0].astype(F32), other[1].astype(F32)
    re, im = (a * c + b * d).astype(BF16), (a * d - b * c).astype(BF16)
    cos, sin = mats[0], mats[1]
    turn_re, turn_im = twiddle[0], twiddle[1]
    u, v = dot(cos, re) + dot(sin, im), dot(cos, im) - dot(sin, re)
    re, im = (u * turn_re + v * turn_im).astype(BF16), (v * turn_re - u * turn_im).astype(BF16)
    cos, sin = mats[2], mats[3]
    scale = kernel[...]
    u, v = dot(re, cos) + dot(im, sin), dot(im, cos) - dot(re, sin)
    re, im = (u * scale).astype(BF16), (v * scale).astype(BF16)
    u, v = dot(re, cos) - dot(im, sin), dot(im, cos) + dot(re, sin)
    re, im = (u * turn_re - v * turn_im).astype(BF16), (v * turn_re + u * turn_im).astype(BF16)
    cos, sin = mats[0], mats[1]
    e, f = dot(cos, re) - dot(sin, im), dot(cos, im) + dot(sin, re)
    return weight * (a * e - b * f), weight * (a * f + b * e)


def kernel_body(
    n_pool, own, occ, kernel, mats, twiddle, out, gram,
    first, second, occ1, occ2, slots, accum, partial,
    pool_send, pool_recv, next_send, next_recv, slot_recv, ring_send, mate_send,
):
    k, band = lax.axis_index("pool"), lax.axis_index("band")
    n_band = 4 * NX
    y, x, core = band // (2 * NX), (band // 2) % NX, band % 2

    def at(yy, xx, cc):
        return yy * (2 * NX) + xx * 2 + cc

    here = k
    ahead, behind = (k + 1) % n_pool, (k + n_pool - 1) % n_pool
    right, left = (x + 1) % NX, (x + NX - 1) % NX
    x_up, x_down = at(y, right, core), at(y, left, core)
    y_mate, mate = at(1 - y, x, core), at(y, x, 1 - core)
    band_up, band_down = (band + 1) % n_band, (band + n_band - 1) % n_band

    barrier = pltpu.get_barrier_semaphore()
    greeted = [(ahead, band), (behind, band)]
    greeted += [(here, b) for b in (band_up, band_down, x_up, x_down, y_mate, mate)]
    for device in greeted:
        pl.semaphore_signal(barrier, inc=1, device_id=device, device_id_type=pl.DeviceIdType.MESH)
    pl.semaphore_wait(barrier, len(greeted))

    started = []

    def send(src, dst, send_sem, recv_sem, device):
        copy = pltpu.make_async_remote_copy(
            src_ref=src, dst_ref=dst, send_sem=send_sem, recv_sem=recv_sem,
            device_id=device, device_id_type=pl.DeviceIdType.MESH,
        )
        copy.start()
        started.append(copy)

    def arrive(dst, recv_sem, send_sem):
        pltpu.make_async_remote_copy(
            src_ref=dst, dst_ref=dst, send_sem=send_sem, recv_sem=recv_sem,
            device_id=(here, band), device_id_type=pl.DeviceIdType.MESH,
        ).wait_recv()

    counts = {"ring": 0, "mate": 0}

    def pass_on(kind, src, slot, part, to):
        sems = ring_send if kind == "ring" else mate_send
        send(src, slots.at[slot, part], sems.at[counts[kind]], slot_recv.at[slot, part], (here, to))
        counts[kind] += 1

    def take(slot, part):
        arrive(slots.at[slot, part], slot_recv.at[slot, part], ring_send.at[0])

    send(occ, occ1, pool_send.at[2], pool_recv.at[2], (ahead, band))
    for part in range(2):
        send(own.at[part], first.at[part], pool_send.at[part], pool_recv.at[part], (ahead, band))
    for part in range(2):
        for to in (x_up, x_down):
            pass_on("ring", own.at[part], band, part, to)
    for part in range(2):
        pass_on("ring", own.at[part], band, part, y_mate)
    for part in range(2):
        pass_on("mate", own.at[part], band, part, mate)

    def relay(slot, part, to):
        take(slot, part)
        for target in to:
            pass_on("mate" if target is mate else "ring", slots.at[slot, part], slot, part, target)

    relay(x_down, 0, (x_up, mate))
    relay(x_up, 1, (x_down, mate))
    relay(x_down, 1, (mate,))
    relay(x_up, 0, (mate,))

    arrive(occ1, pool_recv.at[2], pool_send.at[2])
    send(occ1, occ2, next_send.at[2], next_recv.at[2], (here, band_up))
    for part in range(2):
        arrive(first.at[part], pool_recv.at[part], pool_send.at[part])
        send(first.at[part], second.at[part], next_send.at[part], next_recv.at[part], (here, band_up))

    weight = -0.5 * occ1[...].astype(F32)
    re, im = exchange_pair(own, first, weight, mats, twiddle, kernel)
    accum[0], accum[1] = re, im

    relay(y_mate, 0, (x_up, x_down, mate))
    relay(y_mate, 1, (x_up, x_down, mate))

    arrive(occ2, next_recv.at[2], next_send.at[2])
    for part in range(2):
        arrive(second.at[part], next_recv.at[part], next_send.at[part])
    weight = -0.5 * occ2[...].astype(F32)
    re, im = exchange_pair(own, second, weight, mats, twiddle, kernel)
    re, im = (accum[0] + re).astype(BF16), (accum[1] + im).astype(BF16)
    out[0], out[1] = re, im
    accum[0], accum[1] = re.astype(F32), im.astype(F32)

    other_down, other_up = at(1 - y, left, core), at(1 - y, right, core)
    far, other_far = at(y, (x + 2) % NX, core), at(1 - y, (x + 2) % NX, core)
    relay(other_down, 0, (x_up, mate))
    relay(other_up, 1, (x_down, mate))
    relay(other_down, 1, (mate,))
    relay(other_up, 0, (mate,))
    relay(far, 0, (mate,))
    relay(far, 1, (mate,))

    def overlap(ref, slot):
        c, d = ref[0].astype(F32), ref[1].astype(F32)
        e, f = accum[0], accum[1]
        partial[slot] = (c * e + d * f).reshape(SIDE // 8, 8, SIDE).sum(0)
        partial[slot + n_band] = (c * f - d * e).reshape(SIDE // 8, 8, SIDE).sum(0)

    overlap(own, band)
    for slot in (x_down, x_up, y_mate, other_down, other_up, far):
        overlap(slots.at[slot], slot)
    relay(other_far, 0, (mate,))
    relay(other_far, 1, (mate,))
    overlap(slots.at[other_far], other_far)
    twin = 1 - core
    order = [(y, x), (y, left), (y, right), (1 - y, x), (1 - y, left), (1 - y, right)]
    order += [(y, (x + 2) % NX), (1 - y, (x + 2) % NX)]
    for yy, xx in order:
        slot = at(yy, xx, twin)
        take(slot, 0)
        take(slot, 1)
        overlap(slots.at[slot], slot)

    sums = partial[...].sum(axis=1)
    ones = jnp.full((8, SIDE), 1.0 / math.sqrt(GRID), F32)
    line = lax.dot_general(
        ones, sums, (((1,), (1,)), ((), ())), precision=lax.Precision.HIGHEST, preferred_element_type=F32
    )
    gram[0] = line[0:1, 0:n_band]
    gram[1] = line[0:1, n_band : 2 * n_band]

    for copy in started:
        copy.wait_send()


def shards(n_pool, orbitals, occupation, kernel):
    n_band = 4 * NX
    own = orbitals.reshape(2, SIDE, SIDE)
    scale = (kernel / GRID).reshape(NG, 6, 6, NG).transpose(0, 2, 1, 3).reshape(SIDE, SIDE)
    mats, twiddle = tables()
    vmem = pl.BlockSpec(memory_space=pltpu.VMEM)
    pair = pltpu.VMEM((2, SIDE, SIDE), BF16)
    dma = pltpu.SemaphoreType.DMA
    exchanged, gram = pl.pallas_call(
        functools.partial(kernel_body, n_pool),
        out_shape=(
            jax.ShapeDtypeStruct((2, SIDE, SIDE), BF16),
            jax.ShapeDtypeStruct((2, 1, n_band), F32),
        ),
        in_specs=[vmem, vmem, vmem, vmem, vmem],
        out_specs=(vmem, vmem),
        scratch_shapes=[
            pair, pair, pltpu.VMEM((1, 1), jnp.int32), pltpu.VMEM((1, 1), jnp.int32),
            pltpu.VMEM((n_band, 2, SIDE, SIDE), BF16),
            pltpu.VMEM((2, SIDE, SIDE), F32),
            pltpu.VMEM((2 * n_band, 8, SIDE), F32),
            dma((3,)), dma((3,)), dma((3,)), dma((3,)), dma((n_band, 2)), dma((14,)), dma((16,)),
        ],
        compiler_params=pltpu.CompilerParams(
            collective_id=0, has_side_effects=True, vmem_limit_bytes=50 * 1024 * 1024
        ),
    )(own, occupation, scale, mats, twiddle)
    return exchanged.reshape(1, 1, 2, GRID), gram.reshape(1, 2, n_band, 1)


def solution(mesh):
    return jax.shard_map(
        functools.partial(shards, mesh.shape["pool"]),
        mesh=mesh,
        in_specs=(P("pool", "band", None, None), P("pool", "band"), P()),
        out_specs=(P("pool", "band", None, None), P("pool", None, None, "band")),
        check_vma=False,
    )
```

```python
import functools
import math

import jax
import jax.numpy as jnp
import numpy as np
from jax import lax
from jax.experimental import pallas as pl
from jax.experimental.pallas import tpu as pltpu
from jax.sharding import PartitionSpec as P

NG = 36
GRID = 46656
SIDE = 216
WIDE = 256
DENSE = 368
BLOCK = 1024
FULL = GRID // BLOCK
TAIL = GRID - FULL * BLOCK
NX = 4
F32 = jnp.float32
BF16 = jnp.bfloat16
HALVES = ((0, 23296), (23296, 23360))
QUARTERS = ((0, 11648), (11648, 11648), (23296, 11648), (34944, 11712))


def tables():
    index = np.arange(SIDE)
    x, y_high = index // 6, index % 6
    rows = (np.outer(x, x) + 6 * np.outer(y_high, y_high)) % NG
    y_low, z = index // NG, index % NG
    lanes = (np.outer(z, z) + 6 * np.outer(y_low, y_low)) % NG
    twiddle = np.outer(y_high, y_low) % NG
    step = 2.0 * math.pi / NG

    def both(phases, shape):
        out = np.zeros((2,) + shape, np.float32)
        out[:, :SIDE, :SIDE] = np.stack([np.cos(step * phases), np.sin(step * phases)])
        return jnp.asarray(out)

    return (
        both(rows, (SIDE, SIDE)).astype(BF16),
        both(lanes, (WIDE, WIDE)).astype(BF16),
        both(twiddle, (SIDE, WIDE)),
    )


def dot(a, b):
    return jnp.dot(a, b, preferred_element_type=F32)


def lane_index(rows):
    return lax.broadcasted_iota(jnp.int32, (rows, 128), 1)


def unpack(raw, dense):
    for t in range(FULL):
        dense[:, pl.ds(8 * t, 8), :] = raw[:, pl.ds(BLOCK * t, BLOCK)].astype(F32).reshape(2, 8, 128)
    for j in range(0, TAIL, 128):
        width = min(128, TAIL - j)
        dense[:, 8 * FULL + j // 128, 0:width] = raw[:, pl.ds(FULL * BLOCK + j, width)].astype(F32)


def to_planes(dense, planes):
    for start in range(16):
        count = 14 if start < 8 else 13
        row, shift = (SIDE * start) // 128, (SIDE * start) % 128
        low = dense[pl.ds(row, count, stride=27), :]
        high = dense[pl.ds(row + 1, count, stride=27), :]
        if shift:
            low, high = pltpu.roll(low, 128 - shift, 1), pltpu.roll(high, 128 - shift, 1)
            keep = lane_index(count) < 128 - shift
            low = jnp.where(keep, low, high)
            if shift + SIDE > 256:
                last = pltpu.roll(dense[pl.ds(row + 2, count, stride=27), :], 128 - shift, 1)
                high = jnp.where(keep, high, last)
        planes[0, pl.ds(start, count, stride=16), :] = low
        planes[1, pl.ds(start, count, stride=16), :] = high


def to_dense(planes, dense):
    for q in range(27):
        count = 14 if q <= 12 else 13
        total, lane = None, lane_index(count)
        pos = 0
        while pos < 128:
            row, col = divmod(128 * q + pos, SIDE)
            plane, first = (0, 0) if col < 128 else (1, 128)
            width = min((SIDE if plane else 128) - col, 128 - pos)
            piece = planes[plane, pl.ds(row, count, stride=16), :]
            shift = (pos - (col - first)) % 128
            if shift:
                piece = pltpu.roll(piece, shift, 1)
            total = piece if total is None else jnp.where(lane < pos, total, piece)
            pos += width
        dense[pl.ds(q, count, stride=27), :] = total
    row, col = divmod(364 * 128, SIDE)
    dense[364:365, 0:64] = planes[1, row : row + 1, col - 128 : col - 64]


def permute_scale(planes, scale):
    lane = lane_index(NG)
    for low in range(6):
        for plane in range(2):
            total = jnp.zeros((NG, 128), F32)
            for high in range(6):
                pos, end = max(NG * high, 128 * plane), min(NG * high + NG, 128 * plane + 128)
                while pos < end:
                    col = NG * low + pos - NG * high
                    source = col // 128
                    width = min(end - pos, 128 * (source + 1) - col)
                    piece = planes[source, pl.ds(high, NG, stride=6), :]
                    shift = (pos - col) % 128
                    if shift:
                        piece = pltpu.roll(piece, shift, 1)
                    at = pos - 128 * plane
                    total = jnp.where((lane >= at) & (lane < at + width), piece, total)
                    pos += width
            scale[plane, pl.ds(low, NG, stride=6), :] = total * (1.0 / GRID)


def wide(planes):
    return jnp.concatenate([planes[0], planes[1]], axis=1)


def exchange_pair(own, other, weight, rows, lanes, twiddle, scale):
    c, d, a, b = wide(own.at[0]), wide(own.at[1]), wide(other.at[0]), wide(other.at[1])
    re, im = (a * c + b * d).astype(BF16), (a * d - b * c).astype(BF16)
    cos, sin = rows[0], rows[1]
    turn_re, turn_im = twiddle[0], twiddle[1]
    u, v = dot(cos, re) + dot(sin, im), dot(cos, im) - dot(sin, re)
    re, im = (u * turn_re + v * turn_im).astype(BF16), (v * turn_re - u * turn_im).astype(BF16)
    cos, sin = lanes[0], lanes[1]
    factor = wide(scale)
    u, v = dot(re, cos) + dot(im, sin), dot(im, cos) - dot(re, sin)
    re, im = (u * factor).astype(BF16), (v * factor).astype(BF16)
    u, v = dot(re, cos) - dot(im, sin), dot(im, cos) + dot(re, sin)
    re, im = (u * turn_re - v * turn_im).astype(BF16), (v * turn_re + u * turn_im).astype(BF16)
    cos, sin = rows[0], rows[1]
    e, f = dot(cos, re) - dot(sin, im), dot(cos, im) + dot(sin, re)
    return weight * (a * e - b * f), weight * (a * f + b * e)


def kernel_body(
    n_pool, own, occ, kernel, rows_in, lanes_in, twiddle_in, out, gram,
    first, second, occ1, occ2, slots, flat, rows, lanes, twiddle,
    dense, own_planes, planes, accum, scale, ket, ket_turned, partial,
    local_sem, pool_send, pool_recv, next_send, next_recv, slot_recv, ring_send, mate_send,
):
    k, band = lax.axis_index("pool"), lax.axis_index("band")
    n_band = 4 * NX
    y, x, core = band // (2 * NX), (band // 2) % NX, band % 2

    def at(yy, xx, cc):
        return yy * (2 * NX) + xx * 2 + cc

    ahead, behind = (k + 1) % n_pool, (k + n_pool - 1) % n_pool
    right, left, across = (x + 1) % NX, (x + NX - 1) % NX, (x + 2) % NX
    x_up, x_down = at(y, right, core), at(y, left, core)
    y_mate, mate = at(1 - y, x, core), at(y, x, 1 - core)
    band_up, band_down = (band + 1) % n_band, (band + n_band - 1) % n_band
    mesh_id = pl.DeviceIdType.MESH

    barrier = pltpu.get_barrier_semaphore()
    senders = [(behind, band)] + [(k, b) for b in (band_down, x_up, x_down, y_mate, mate)]
    for device in senders:
        pl.semaphore_signal(barrier, inc=1, device_id=device, device_id_type=mesh_id)

    local = [
        pltpu.make_async_copy(src, dst, local_sem.at[i])
        for i, (src, dst) in enumerate(
            [(own, slots.at[band]), (kernel, flat), (rows_in, rows), (lanes_in, lanes), (twiddle_in, twiddle)]
        )
    ]
    for copy in local:
        copy.start()
    pl.semaphore_wait(barrier, len(senders))

    def remote(src, dst, send_sem, recv_sem, device):
        return pltpu.make_async_remote_copy(
            src_ref=src, dst_ref=dst, send_sem=send_sem, recv_sem=recv_sem, device_id=device, device_id_type=mesh_id
        )

    def piece(ref, span):
        return ref.at[:, pl.ds(span[0], span[1])]

    def ring(index, src, slot, part, to):
        span = HALVES[part]
        return remote(
            piece(src, span), piece(slots.at[slot], span), ring_send.at[index], slot_recv.at[slot, part], (k, to)
        )

    def to_mate(index, src, slot, part):
        span = HALVES[part]
        return remote(
            piece(src, span), piece(slots.at[slot], span), mate_send.at[index], slot_recv.at[slot, part], (k, mate)
        )

    def take(slot, part):
        ring(0, slots.at[slot], slot, part, band).wait_recv()

    other_down, other_up = at(1 - y, left, core), at(1 - y, right, core)
    far, other_far = at(y, across, core), at(1 - y, across, core)

    pool = [remote(occ, occ1, pool_send.at[4], pool_recv.at[4], (ahead, band))]
    pool += [
        remote(piece(own, span), piece(first, span), pool_send.at[i], pool_recv.at[i], (ahead, band))
        for i, span in enumerate(QUARTERS)
    ]
    onward = [remote(occ1, occ2, next_send.at[4], next_recv.at[4], (k, band_up))]
    onward += [
        remote(piece(first, span), piece(second, span), next_send.at[i], next_recv.at[i], (k, band_up))
        for i, span in enumerate(QUARTERS)
    ]
    ring_own = [
        ring(0, own, band, 0, x_up), ring(1, own, band, 1, x_down), ring(2, own, band, 1, x_up),
        ring(3, own, band, 0, x_down), ring(4, own, band, 0, y_mate), ring(5, own, band, 1, y_mate),
    ]
    mate_own = [to_mate(0, own, band, 0), to_mate(1, own, band, 1)]
    relays = [
        (x_down, 0, [ring(6, slots.at[x_down], x_down, 0, x_up)]),
        (x_up, 1, [ring(7, slots.at[x_up], x_up, 1, x_down)]),
        (x_down, 1, []),
        (x_up, 0, []),
        (y_mate, 0, [ring(8, slots.at[y_mate], y_mate, 0, x_up), ring(9, slots.at[y_mate], y_mate, 0, x_down)]),
        (y_mate, 1, [ring(10, slots.at[y_mate], y_mate, 1, x_up), ring(11, slots.at[y_mate], y_mate, 1, x_down)]),
        (far, 0, [ring(12, slots.at[far], far, 0, y_mate)]),
        (far, 1, [ring(13, slots.at[far], far, 1, y_mate)]),
        (other_down, 0, []), (other_down, 1, []), (other_up, 0, []), (other_up, 1, []),
        (other_far, 0, []), (other_far, 1, []),
    ]
    relays = [
        (slot, part, copies + [to_mate(2 + i, slots.at[slot], slot, part)])
        for i, (slot, part, copies) in enumerate(relays)
    ]

    def relay(*which):
        for i in which:
            slot, part, copies = relays[i]
            take(slot, part)
            for copy in copies:
                copy.start()

    def start(copies):
        for copy in copies:
            copy.start()

    start(pool)
    start(ring_own)
    start(mate_own)

    for copy in local:
        copy.wait()
    dense[:, pl.ds(360, 8), :] = jnp.zeros((2, 8, 128), F32)
    for t in range(FULL):
        dense[0, pl.ds(8 * t, 8), :] = flat[pl.ds(BLOCK * t, BLOCK)].reshape(8, 128)
    for j in range(0, TAIL, 128):
        width = min(128, TAIL - j)
        dense[0, 8 * FULL + j // 128, 0:width] = flat[pl.ds(FULL * BLOCK + j, width)]
    to_planes(dense.at[0], planes.at[0])
    permute_scale(planes.at[0], scale)
    unpack(slots.at[band], dense)
    for part in range(2):
        to_planes(dense.at[part], own_planes.at[part])
    partial[...] = jnp.zeros(partial.shape, F32)

    early = k < 2

    @pl.when(early)
    def _():
        relay(*range(14))

    @pl.when(jnp.logical_not(early))
    def _():
        relay(0, 1, 2, 3)

    for arrived, copy in zip(pool, onward):
        arrived.wait_recv()
        copy.start()

    def pair(raw, occupied):
        unpack(raw, dense)
        for part in range(2):
            to_planes(dense.at[part], planes.at[part])
        weight = -0.5 * occupied[...].astype(F32)
        return exchange_pair(own_planes, planes, weight, rows, lanes, twiddle, scale)

    @pl.when(jnp.logical_not(early))
    def _():
        relay(4, 5, 6, 7)

    re, im = pair(first, occ1)
    for part, value in enumerate((re, im)):
        accum[part, 0], accum[part, 1] = value[:, :128], value[:, 128:]

    for copy in onward:
        copy.wait_recv()
    re, im = pair(second, occ2)
    for part, value in enumerate((re, im)):
        accum[part, 0] += value[:, :128]
        accum[part, 1] += value[:, 128:]

    @pl.when(jnp.logical_not(early))
    def _():
        relay(*range(8, 14))

    for part in range(2):
        to_dense(accum.at[part], dense.at[part])

    def emit(start_at, width, value):
        span = pl.ds(start_at, width)
        value = value.astype(BF16)
        out[:, span] = value
        ket[:, span] = value.astype(F32)

    def emit_turned(start_at, width, value):
        ket_turned[:, pl.ds(start_at, width)] = value.astype(BF16).astype(F32)

    for t in range(FULL):
        both = dense[:, pl.ds(8 * t, 8), :]
        turned = jnp.concatenate([both[1:2], -both[0:1]], axis=0)
        emit(BLOCK * t, BLOCK, both.reshape(2, BLOCK))
        emit_turned(BLOCK * t, BLOCK, turned.reshape(2, BLOCK))
    for j in range(0, TAIL, 128):
        width = min(128, TAIL - j)
        both = dense[:, 8 * FULL + j // 128, 0:width]
        emit(FULL * BLOCK + j, width, both)
        emit_turned(FULL * BLOCK + j, width, jnp.concatenate([both[1:2], -both[0:1]], axis=0))

    def overlap(slot):
        for index, side in ((slot, ket), (slot + n_band, ket_turned)):
            total = jnp.zeros((2, BLOCK), F32)
            for t in range(FULL):
                span = pl.ds(BLOCK * t, BLOCK)
                total += slots[slot, :, span].astype(F32) * side[:, span]
            fold = total[:, 0:128]
            for j in range(1, BLOCK // 128):
                fold += total[:, 128 * j : 128 * j + 128]
            for j in range(0, TAIL - 64, 128):
                span = pl.ds(FULL * BLOCK + j, 128)
                fold += slots[slot, :, span].astype(F32) * side[:, span]
            span = pl.ds(GRID - 64, 64)
            partial[index, 0:2, :] = fold
            partial[index, 2:4, 0:64] = slots[slot, :, span].astype(F32) * side[:, span]

    def same(j, carry):
        overlap(at((y + j // NX) % 2, (x + j) % NX, core))
        return carry

    def twin(j, carry):
        slot = at((y + j // NX) % 2, (x + j) % NX, 1 - core)
        for part in range(2):
            take(slot, part)
        overlap(slot)
        return carry

    lax.fori_loop(0, 2 * NX, same, 0)
    lax.fori_loop(0, 2 * NX, twin, 0)

    sums = partial[...].sum(axis=1)
    ones = jnp.full((8, 128), 1.0 / math.sqrt(GRID), F32)
    line = lax.dot_general(
        ones, sums, (((1,), (1,)), ((), ())), precision=lax.Precision.HIGHEST, preferred_element_type=F32
    )
    gram[0] = line[0:1, 0:n_band]
    gram[1] = line[0:1, n_band : 2 * n_band]

    for copy in pool + onward + ring_own + mate_own:
        copy.wait_send()
    for _, _, copies in relays:
        for copy in copies:
            copy.wait_send()


def shards(n_pool, orbitals, occupation, kernel):
    n_band = 4 * NX
    vmem = pl.BlockSpec(memory_space=pltpu.VMEM)
    hbm = pl.BlockSpec(memory_space=pltpu.HBM)
    raw = pltpu.VMEM((2, GRID), BF16)
    dma = pltpu.SemaphoreType.DMA
    scalar = pltpu.VMEM((1, 1), jnp.int32)
    plane = pltpu.VMEM((2, 2, SIDE, 128), F32)
    exchanged, gram = pl.pallas_call(
        functools.partial(kernel_body, n_pool),
        out_shape=(
            jax.ShapeDtypeStruct((2, GRID), BF16),
            jax.ShapeDtypeStruct((2, 1, n_band), F32),
        ),
        in_specs=[hbm, vmem, hbm, hbm, hbm, hbm],
        out_specs=(vmem, vmem),
        scratch_shapes=[
            raw, raw, scalar, scalar,
            pltpu.VMEM((n_band, 2, GRID), BF16),
            pltpu.VMEM((GRID,), F32),
            pltpu.VMEM((2, SIDE, SIDE), BF16),
            pltpu.VMEM((2, WIDE, WIDE), BF16),
            pltpu.VMEM((2, SIDE, WIDE), F32),
            pltpu.VMEM((2, DENSE, 128), F32),
            plane, plane, plane,
            pltpu.VMEM((2, SIDE, 128), F32),
            pltpu.VMEM((2, GRID), F32),
            pltpu.VMEM((2, GRID), F32),
            pltpu.VMEM((2 * n_band, 8, 128), F32),
            dma((5,)), dma((5,)), dma((5,)), dma((5,)), dma((5,)), dma((n_band, 2)), dma((14,)), dma((16,)),
        ],
        compiler_params=pltpu.CompilerParams(
            collective_id=0, has_side_effects=True, vmem_limit_bytes=67043328
        ),
    )(orbitals.reshape(2, GRID), occupation, kernel, *tables())
    return exchanged.reshape(1, 1, 2, GRID), gram.reshape(1, 2, n_band, 1)


def solution(mesh):
    return jax.shard_map(
        functools.partial(shards, mesh.shape["pool"]),
        mesh=mesh,
        in_specs=(P("pool", "band", None, None), P("pool", "band"), P()),
        out_specs=(P("pool", "band", None, None), P("pool", None, None, "band")),
        check_vma=False,
    )
```

```python
import functools
import math
import jax
import jax.numpy as jnp
import numpy as np
from jax import lax
from jax.experimental import pallas as pl
from jax.experimental.pallas import tpu as pltpu
from jax.sharding import PartitionSpec as P
NG = 36
GRID = 46656
SIDE = 216
WIDE = 256
DENSE = 368
BLOCK = 1024
FULL = GRID // BLOCK
TAIL = GRID - FULL * BLOCK
NX = 4
WAYS = 4
ROOM = 50331648
F32 = jnp.float32
BF16 = jnp.bfloat16
HALVES = ((0, 23296), (23296, 23360))
QUARTERS = ((0, 11648), (11648, 11648), (23296, 11648), (34944, 11712))

def tables():
    index = np.arange(SIDE)
    x, y_high = (index // 6, index % 6)
    rows = (np.outer(x, x) + 6 * np.outer(y_high, y_high)) % NG
    y_low, z = (index // NG, index % NG)
    lanes = (np.outer(z, z) + 6 * np.outer(y_low, y_low)) % NG
    twiddle = np.outer(y_high, y_low) % NG
    step = 2.0 * math.pi / NG

    def both(phases, shape):
        out = np.zeros((2,) + shape, np.float32)
        out[:, :SIDE, :SIDE] = np.stack([np.cos(step * phases), np.sin(step * phases)])
        return jnp.asarray(out)
    return (both(rows, (SIDE, SIDE)).astype(BF16), both(lanes, (WIDE, WIDE)).astype(BF16), both(twiddle, (SIDE, WIDE)))

def dot(a, b):
    return jnp.dot(a, b, preferred_element_type=F32)

def lane_index(rows):
    return lax.broadcasted_iota(jnp.int32, (rows, 128), 1)

def unpack(raw, dense):
    for t in range(FULL):
        dense[:, pl.ds(8 * t, 8), :] = raw[:, pl.ds(BLOCK * t, BLOCK)].astype(F32).reshape(2, 8, 128)
    for j in range(0, TAIL, 128):
        width = min(128, TAIL - j)
        dense[:, 8 * FULL + j // 128, 0:width] = raw[:, pl.ds(FULL * BLOCK + j, width)].astype(F32)

def to_planes(dense, planes):
    for start in range(16):
        count = 14 if start < 8 else 13
        row, shift = (SIDE * start // 128, SIDE * start % 128)
        low = dense[pl.ds(row, count, stride=27), :]
        high = dense[pl.ds(row + 1, count, stride=27), :]
        if shift:
            low, high = (pltpu.roll(low, 128 - shift, 1), pltpu.roll(high, 128 - shift, 1))
            keep = lane_index(count) < 128 - shift
            low = jnp.where(keep, low, high)
            if shift + SIDE > 256:
                last = pltpu.roll(dense[pl.ds(row + 2, count, stride=27), :], 128 - shift, 1)
                high = jnp.where(keep, high, last)
        planes[0, pl.ds(start, count, stride=16), :] = low
        planes[1, pl.ds(start, count, stride=16), :] = high

def to_dense(planes, dense):
    for q in range(27):
        count = 14 if q <= 12 else 13
        total, lane = (None, lane_index(count))
        pos = 0
        while pos < 128:
            row, col = divmod(128 * q + pos, SIDE)
            plane, first = (0, 0) if col < 128 else (1, 128)
            width = min((SIDE if plane else 128) - col, 128 - pos)
            piece = planes[plane, pl.ds(row, count, stride=16), :]
            shift = (pos - (col - first)) % 128
            if shift:
                piece = pltpu.roll(piece, shift, 1)
            total = piece if total is None else jnp.where(lane < pos, total, piece)
            pos += width
        dense[pl.ds(q, count, stride=27), :] = total
    row, col = divmod(364 * 128, SIDE)
    dense[364:365, 0:64] = planes[1, row:row + 1, col - 128:col - 64]

def permute_scale(planes, scale):
    lane = lane_index(NG)
    for low in range(6):
        for plane in range(2):
            total = jnp.zeros((NG, 128), F32)
            for high in range(6):
                pos, end = (max(NG * high, 128 * plane), min(NG * high + NG, 128 * plane + 128))
                while pos < end:
                    col = NG * low + pos - NG * high
                    source = col // 128
                    width = min(end - pos, 128 * (source + 1) - col)
                    piece = planes[source, pl.ds(high, NG, stride=6), :]
                    shift = (pos - col) % 128
                    if shift:
                        piece = pltpu.roll(piece, shift, 1)
                    at = pos - 128 * plane
                    total = jnp.where((lane >= at) & (lane < at + width), piece, total)
                    pos += width
            scale[plane, pl.ds(low, NG, stride=6), :] = total * (1.0 / GRID)

def wide(planes):
    return jnp.concatenate([planes[0], planes[1]], axis=1)

def exchange_pair(own, other, weight, rows, lanes, twiddle, scale):
    c, d, a, b = (wide(own.at[0]), wide(own.at[1]), wide(other.at[0]), wide(other.at[1]))
    re, im = ((a * c + b * d).astype(BF16), (a * d - b * c).astype(BF16))
    cos, sin = (rows[0], rows[1])
    turn_re, turn_im = (twiddle[0], twiddle[1])
    u, v = (dot(cos, re) + dot(sin, im), dot(cos, im) - dot(sin, re))
    re, im = ((u * turn_re + v * turn_im).astype(BF16), (v * turn_re - u * turn_im).astype(BF16))
    cos, sin = (lanes[0], lanes[1])
    factor = wide(scale)
    u, v = (dot(re, cos) + dot(im, sin), dot(im, cos) - dot(re, sin))
    re, im = ((u * factor).astype(BF16), (v * factor).astype(BF16))
    u, v = (dot(re, cos) - dot(im, sin), dot(im, cos) + dot(re, sin))
    re, im = ((u * turn_re - v * turn_im).astype(BF16), (v * turn_re + u * turn_im).astype(BF16))
    cos, sin = (rows[0], rows[1])
    e, f = (dot(cos, re) - dot(sin, im), dot(cos, im) + dot(sin, re))
    return (weight * (a * e - b * f), weight * (a * f + b * e))

def kernel_body(n_pool, own, occ, kernel, rows_in, lanes_in, twiddle_in, accum, slots, first, second, occ1, occ2, flat, rows, lanes, twiddle, dense, own_planes, planes, scale, local_sem, pool_send, pool_recv, next_send, next_recv, slot_recv, ring_send, mate_send):
    k, band = (lax.axis_index('pool'), lax.axis_index('band'))
    n_band = 4 * NX
    y, x, core = (band // (2 * NX), band // 2 % NX, band % 2)

    def at(yy, xx, cc):
        return yy * (2 * NX) + xx * 2 + cc
    ahead, behind = ((k + 1) % n_pool, (k + n_pool - 1) % n_pool)
    right, left, across = ((x + 1) % NX, (x + NX - 1) % NX, (x + 2) % NX)
    x_up, x_down = (at(y, right, core), at(y, left, core))
    y_mate, mate = (at(1 - y, x, core), at(y, x, 1 - core))
    band_up, band_down = ((band + 1) % n_band, (band + n_band - 1) % n_band)
    mesh_id = pl.DeviceIdType.MESH
    barrier = pltpu.get_barrier_semaphore()
    senders = [(behind, band)] + [(k, b) for b in (band_down, x_up, x_down, y_mate, mate)]
    for device in senders:
        pl.semaphore_signal(barrier, inc=1, device_id=device, device_id_type=mesh_id)
    local = [pltpu.make_async_copy(src, dst, local_sem.at[i]) for i, (src, dst) in enumerate([(own, slots.at[band]), (kernel, flat), (rows_in, rows), (lanes_in, lanes), (twiddle_in, twiddle)])]
    for copy in local:
        copy.start()
    pl.semaphore_wait(barrier, len(senders))

    def remote(src, dst, send_sem, recv_sem, device):
        return pltpu.make_async_remote_copy(src_ref=src, dst_ref=dst, send_sem=send_sem, recv_sem=recv_sem, device_id=device, device_id_type=mesh_id)

    def piece(ref, span):
        return ref.at[:, pl.ds(span[0], span[1])]

    def ring(index, src, slot, part, to):
        span = HALVES[part]
        return remote(piece(src, span), piece(slots.at[slot], span), ring_send.at[index], slot_recv.at[slot, part], (k, to))

    def to_mate(index, src, slot, part):
        span = HALVES[part]
        return remote(piece(src, span), piece(slots.at[slot], span), mate_send.at[index], slot_recv.at[slot, part], (k, mate))

    def take(slot, part):
        ring(0, slots.at[slot], slot, part, band).wait_recv()
    other_down, other_up = (at(1 - y, left, core), at(1 - y, right, core))
    far, other_far = (at(y, across, core), at(1 - y, across, core))
    pool = [remote(occ, occ1, pool_send.at[4], pool_recv.at[4], (ahead, band))]
    pool += [remote(piece(own, span), piece(first, span), pool_send.at[i], pool_recv.at[i], (ahead, band)) for i, span in enumerate(QUARTERS)]
    onward = [remote(occ1, occ2, next_send.at[4], next_recv.at[4], (k, band_up))]
    onward += [remote(piece(first, span), piece(second, span), next_send.at[i], next_recv.at[i], (k, band_up)) for i, span in enumerate(QUARTERS)]
    ring_own = [ring(0, own, band, 0, x_up), ring(1, own, band, 1, x_down), ring(2, own, band, 1, x_up), ring(3, own, band, 0, x_down), ring(4, own, band, 0, y_mate), ring(5, own, band, 1, y_mate)]
    mate_own = [to_mate(0, own, band, 0), to_mate(1, own, band, 1)]
    relays = [(x_down, 0, [ring(6, slots.at[x_down], x_down, 0, x_up)]), (x_up, 1, [ring(7, slots.at[x_up], x_up, 1, x_down)]), (x_down, 1, []), (x_up, 0, []), (y_mate, 0, [ring(8, slots.at[y_mate], y_mate, 0, x_up), ring(9, slots.at[y_mate], y_mate, 0, x_down)]), (y_mate, 1, [ring(10, slots.at[y_mate], y_mate, 1, x_up), ring(11, slots.at[y_mate], y_mate, 1, x_down)]), (far, 0, [ring(12, slots.at[far], far, 0, y_mate)]), (far, 1, [ring(13, slots.at[far], far, 1, y_mate)]), (other_down, 0, []), (other_down, 1, []), (other_up, 0, []), (other_up, 1, []), (other_far, 0, []), (other_far, 1, [])]
    relays = [(slot, part, copies + [to_mate(2 + i, slots.at[slot], slot, part)]) for i, (slot, part, copies) in enumerate(relays)]

    def relay(*which):
        for i in which:
            slot, part, copies = relays[i]
            take(slot, part)
            for copy in copies:
                copy.start()
    twins = [(at(yy, xx, 1 - core), part) for yy in (y, 1 - y) for xx in (x, left, right, across) for part in range(2)]

    def start(copies):
        for copy in copies:
            copy.start()
    start(pool)
    start(ring_own)
    start(mate_own)
    for copy in local:
        copy.wait()
    dense[:, pl.ds(360, 8), :] = jnp.zeros((2, 8, 128), F32)
    for t in range(FULL):
        dense[0, pl.ds(8 * t, 8), :] = flat[pl.ds(BLOCK * t, BLOCK)].reshape(8, 128)
    for j in range(0, TAIL, 128):
        width = min(128, TAIL - j)
        dense[0, 8 * FULL + j // 128, 0:width] = flat[pl.ds(FULL * BLOCK + j, width)]
    to_planes(dense.at[0], planes.at[0])
    permute_scale(planes.at[0], scale)
    unpack(slots.at[band], dense)
    for part in range(2):
        to_planes(dense.at[part], own_planes.at[part])
    early = k == 0

    @pl.when(early)
    def _():
        relay(*range(8))

    @pl.when(jnp.logical_not(early))
    def _():
        relay(0, 1, 2, 3)
    for arrived, copy in zip(pool, onward):
        arrived.wait_recv()
        copy.start()

    def pair(raw, occupied):
        unpack(raw, dense)
        for part in range(2):
            to_planes(dense.at[part], planes.at[part])
        weight = -0.5 * occupied[...].astype(F32)
        return exchange_pair(own_planes, planes, weight, rows, lanes, twiddle, scale)

    @pl.when(jnp.logical_not(early))
    def _():
        relay(*(4, 5, 6, 7))
    re, im = pair(first, occ1)
    for part, value in enumerate((re, im)):
        accum[part, 0], accum[part, 1] = (value[:, :128], value[:, 128:])
    for copy in onward:
        copy.wait_recv()
    re, im = pair(second, occ2)
    for part, value in enumerate((re, im)):
        accum[part, 0] += value[:, :128]
        accum[part, 1] += value[:, 128:]
    relay(*range(8, 14))
    for slot, part in twins:
        take(slot, part)
    for copy in pool:
        copy.wait_send()
    for copy in onward + ring_own + mate_own:
        copy.wait_send()
    for _, _, copies in relays:
        for copy in copies:
            copy.wait_send()

def finish_body(accum, slots, out_hbm, gram, out, dense, ket, ket_turned, partial, sem):
    n_band = slots.shape[0]
    for part in range(2):
        to_dense(accum.at[part], dense.at[part])
    partial[...] = jnp.zeros(partial.shape, F32)

    def emit(start_at, width, value):
        span = pl.ds(start_at, width)
        value = value.astype(BF16)
        out[:, span] = value
        ket[:, span] = value.astype(F32)

    def emit_turned(start_at, width, value):
        ket_turned[:, pl.ds(start_at, width)] = value.astype(BF16).astype(F32)
    for t in range(FULL):
        both = dense[:, pl.ds(8 * t, 8), :]
        turned = jnp.concatenate([both[1:2], -both[0:1]], axis=0)
        emit(BLOCK * t, BLOCK, both.reshape(2, BLOCK))
        emit_turned(BLOCK * t, BLOCK, turned.reshape(2, BLOCK))
    for j in range(0, TAIL, 128):
        width = min(128, TAIL - j)
        both = dense[:, 8 * FULL + j // 128, 0:width]
        emit(FULL * BLOCK + j, width, both)
        emit_turned(FULL * BLOCK + j, width, jnp.concatenate([both[1:2], -both[0:1]], axis=0))
    result = pltpu.make_async_copy(out, out_hbm, sem)
    result.start()

    def overlap(step, carry):
        pair = [2 * step, 2 * step + 1]
        totals = [[jnp.zeros((2, BLOCK), F32) for _ in range(WAYS)] for _ in range(4)]
        for t in range(FULL):
            span = pl.ds(BLOCK * t, BLOCK)
            sides = (ket[:, span], ket_turned[:, span])
            for s, slot in enumerate(pair):
                value = slots[slot, :, span].astype(F32)
                for i, side in enumerate(sides):
                    totals[2 * s + i][t % WAYS] += value * side
        for s, slot in enumerate(pair):
            for i, side in enumerate((ket, ket_turned)):
                index = slot + n_band * i
                total = sum(totals[2 * s + i][1:], totals[2 * s + i][0])
                fold = total[:, 0:128]
                for j in range(1, BLOCK // 128):
                    fold += total[:, 128 * j:128 * j + 128]
                for j in range(0, TAIL - 64, 128):
                    span = pl.ds(FULL * BLOCK + j, 128)
                    fold += slots[slot, :, span].astype(F32) * side[:, span]
                span = pl.ds(GRID - 64, 64)
                partial[index, 0:2, :] = fold
                partial[index, 2:4, 0:64] = slots[slot, :, span].astype(F32) * side[:, span]
        return carry
    lax.fori_loop(0, n_band // 2, overlap, 0)
    sums = partial[...].sum(axis=1)
    ones = jnp.full((8, 128), 1.0 / math.sqrt(GRID), F32)
    line = lax.dot_general(ones, sums, (((1,), (1,)), ((), ())), precision=lax.Precision.HIGHEST, preferred_element_type=F32)
    gram[0] = line[0:1, 0:n_band]
    gram[1] = line[0:1, n_band:2 * n_band]
    result.wait()

def pin(value):
    return pltpu.with_memory_space_constraint(value, pltpu.HBM)

def shards(n_pool, orbitals, occupation, kernel):
    n_band = 4 * NX
    vmem = pl.BlockSpec(memory_space=pltpu.VMEM)
    hbm = pl.BlockSpec(memory_space=pltpu.HBM)
    raw = pltpu.VMEM((2, GRID), BF16)
    dma = pltpu.SemaphoreType.DMA
    scalar = pltpu.VMEM((1, 1), jnp.int32)
    plane = pltpu.VMEM((2, 2, SIDE, 128), F32)
    accum, slots = pl.pallas_call(functools.partial(kernel_body, n_pool), out_shape=(jax.ShapeDtypeStruct((2, 2, SIDE, 128), F32), jax.ShapeDtypeStruct((n_band, 2, GRID), BF16)), in_specs=[hbm] * 6, out_specs=(vmem, vmem), scratch_shapes=[raw, raw, scalar, scalar, pltpu.VMEM((GRID,), F32), pltpu.VMEM((2, SIDE, SIDE), BF16), pltpu.VMEM((2, WIDE, WIDE), BF16), pltpu.VMEM((2, SIDE, WIDE), F32), pltpu.VMEM((2, DENSE, 128), F32), plane, plane, pltpu.VMEM((2, SIDE, 128), F32), dma((5,)), dma((5,)), dma((5,)), dma((5,)), dma((5,)), dma((n_band, 2)), dma((14,)), dma((16,))], compiler_params=pltpu.CompilerParams(collective_id=0, has_side_effects=True, vmem_limit_bytes=ROOM), name='exchange')(pin(orbitals.reshape(2, GRID)), occupation, *map(pin, (kernel, *tables())))
    exchanged, gram = pl.pallas_call(finish_body, out_shape=(jax.ShapeDtypeStruct((2, GRID), BF16), jax.ShapeDtypeStruct((2, 1, n_band), F32)), in_specs=[vmem, vmem], out_specs=(hbm, vmem), scratch_shapes=[raw, pltpu.VMEM((2, DENSE, 128), F32), pltpu.VMEM((2, GRID), F32), pltpu.VMEM((2, GRID), F32), pltpu.VMEM((2 * n_band, 8, 128), F32), dma], compiler_params=pltpu.CompilerParams(vmem_limit_bytes=16 * 1024 * 1024), name='finish')(accum, slots)
    return (exchanged.reshape(1, 1, 2, GRID), gram.reshape(1, 2, n_band, 1))

def solution(mesh):
    return jax.shard_map(functools.partial(shards, mesh.shape['pool']), mesh=mesh, in_specs=(P('pool', 'band', None, None), P('pool', 'band'), P()), out_specs=(P('pool', 'band', None, None), P('pool', None, None, 'band')), check_vma=False)
```

```python
import functools
import math
import jax
import jax.numpy as jnp
import numpy as np
from jax import lax
from jax.experimental import pallas as pl
from jax.experimental.pallas import tpu as pltpu
from jax.sharding import PartitionSpec as P
NG = 36
GRID = 46656
SIDE = 216
WIDE = 256
DENSE = 368
BLOCK = 1024
FULL = GRID // BLOCK
TAIL = GRID - FULL * BLOCK
NX = 4
WAYS = 4
ROOM = 50331648
F32 = jnp.float32
BF16 = jnp.bfloat16
HALVES = ((0, 23296), (23296, 23360))
QUARTERS = ((0, 11648), (11648, 11648), (23296, 11648), (34944, 11712))

def tables():
    index = np.arange(SIDE)
    x, y_high = (index // 6, index % 6)
    rows = (np.outer(x, x) + 6 * np.outer(y_high, y_high)) % NG
    y_low, z = (index // NG, index % NG)
    lanes = (np.outer(z, z) + 6 * np.outer(y_low, y_low)) % NG
    twiddle = np.outer(y_high, y_low) % NG
    step = 2.0 * math.pi / NG

    def both(phases, shape):
        out = np.zeros((2,) + shape, np.float32)
        out[:, :SIDE, :SIDE] = np.stack([np.cos(step * phases), np.sin(step * phases)])
        return jnp.asarray(out)
    return (both(rows, (SIDE, SIDE)).astype(BF16), both(lanes, (WIDE, WIDE)).astype(BF16), both(twiddle, (SIDE, WIDE)))

def dot(a, b):
    return jnp.dot(a, b, preferred_element_type=F32)

def lane_index(rows):
    return lax.broadcasted_iota(jnp.int32, (rows, 128), 1)

def unpack(raw, dense):
    for t in range(FULL):
        dense[:, pl.ds(8 * t, 8), :] = raw[:, pl.ds(BLOCK * t, BLOCK)].astype(F32).reshape(2, 8, 128)
    for j in range(0, TAIL, 128):
        width = min(128, TAIL - j)
        dense[:, 8 * FULL + j // 128, 0:width] = raw[:, pl.ds(FULL * BLOCK + j, width)].astype(F32)

def to_planes(dense, planes):
    for start in range(16):
        count = 14 if start < 8 else 13
        row, shift = (SIDE * start // 128, SIDE * start % 128)
        low = dense[pl.ds(row, count, stride=27), :]
        high = dense[pl.ds(row + 1, count, stride=27), :]
        if shift:
            low, high = (pltpu.roll(low, 128 - shift, 1), pltpu.roll(high, 128 - shift, 1))
            keep = lane_index(count) < 128 - shift
            low = jnp.where(keep, low, high)
            if shift + SIDE > 256:
                last = pltpu.roll(dense[pl.ds(row + 2, count, stride=27), :], 128 - shift, 1)
                high = jnp.where(keep, high, last)
        planes[0, pl.ds(start, count, stride=16), :] = low
        planes[1, pl.ds(start, count, stride=16), :] = high

def to_dense(planes, dense):
    for q in range(27):
        count = 14 if q <= 12 else 13
        total, lane = (None, lane_index(count))
        pos = 0
        while pos < 128:
            row, col = divmod(128 * q + pos, SIDE)
            plane, first = (0, 0) if col < 128 else (1, 128)
            width = min((SIDE if plane else 128) - col, 128 - pos)
            piece = planes[plane, pl.ds(row, count, stride=16), :]
            shift = (pos - (col - first)) % 128
            if shift:
                piece = pltpu.roll(piece, shift, 1)
            total = piece if total is None else jnp.where(lane < pos, total, piece)
            pos += width
        dense[pl.ds(q, count, stride=27), :] = total
    row, col = divmod(364 * 128, SIDE)
    dense[364:365, 0:64] = planes[1, row:row + 1, col - 128:col - 64]

def permute_scale(planes, scale):
    lane = lane_index(NG)
    for low in range(6):
        for plane in range(2):
            total = jnp.zeros((NG, 128), F32)
            for high in range(6):
                pos, end = (max(NG * high, 128 * plane), min(NG * high + NG, 128 * plane + 128))
                while pos < end:
                    col = NG * low + pos - NG * high
                    source = col // 128
                    width = min(end - pos, 128 * (source + 1) - col)
                    piece = planes[source, pl.ds(high, NG, stride=6), :]
                    shift = (pos - col) % 128
                    if shift:
                        piece = pltpu.roll(piece, shift, 1)
                    at = pos - 128 * plane
                    total = jnp.where((lane >= at) & (lane < at + width), piece, total)
                    pos += width
            scale[plane, pl.ds(low, NG, stride=6), :] = total * (1.0 / GRID)

def wide(planes):
    return jnp.concatenate([planes[0], planes[1]], axis=1)

def exchange_pair(own, other, weight, rows, lanes, twiddle, scale):
    c, d, a, b = (wide(own.at[0]), wide(own.at[1]), wide(other.at[0]), wide(other.at[1]))
    re, im = ((a * c + b * d).astype(BF16), (a * d - b * c).astype(BF16))
    cos, sin = (rows[0], rows[1])
    turn_re, turn_im = (twiddle[0], twiddle[1])
    u, v = (dot(cos, re) + dot(sin, im), dot(cos, im) - dot(sin, re))
    re, im = ((u * turn_re + v * turn_im).astype(BF16), (v * turn_re - u * turn_im).astype(BF16))
    cos, sin = (lanes[0], lanes[1])
    factor = wide(scale)
    u, v = (dot(re, cos) + dot(im, sin), dot(im, cos) - dot(re, sin))
    re, im = ((u * factor).astype(BF16), (v * factor).astype(BF16))
    u, v = (dot(re, cos) - dot(im, sin), dot(im, cos) + dot(re, sin))
    re, im = ((u * turn_re - v * turn_im).astype(BF16), (v * turn_re + u * turn_im).astype(BF16))
    cos, sin = (rows[0], rows[1])
    e, f = (dot(cos, re) - dot(sin, im), dot(cos, im) + dot(sin, re))
    return (weight * (a * e - b * f), weight * (a * f + b * e))

def kernel_body(n_pool, own, occ, kernel, rows_in, lanes_in, twiddle_in, accum, slots, first, second, occ1, occ2, flat, rows, lanes, twiddle, dense, own_planes, planes, scale, local_sem, pool_send, pool_recv, next_send, next_recv, slot_recv, ring_send, mate_send):
    k, band = (lax.axis_index('pool'), lax.axis_index('band'))
    n_band = 4 * NX
    y, x, core = (band // (2 * NX), band // 2 % NX, band % 2)

    def at(yy, xx, cc):
        return yy * (2 * NX) + xx * 2 + cc
    ahead, behind = ((k + 1) % n_pool, (k + n_pool - 1) % n_pool)
    right, left, across = ((x + 1) % NX, (x + NX - 1) % NX, (x + 2) % NX)
    x_up, x_down = (at(y, right, core), at(y, left, core))
    y_mate, mate = (at(1 - y, x, core), at(y, x, 1 - core))
    band_up, band_down = ((band + 1) % n_band, (band + n_band - 1) % n_band)
    mesh_id = pl.DeviceIdType.MESH
    barrier = pltpu.get_barrier_semaphore()
    senders = [(behind, band)] + [(k, b) for b in (band_down, x_up, x_down, y_mate, mate)]
    for device in senders:
        pl.semaphore_signal(barrier, inc=1, device_id=device, device_id_type=mesh_id)
    local = [pltpu.make_async_copy(src, dst, local_sem.at[i]) for i, (src, dst) in enumerate([(own, slots.at[band]), (kernel, flat), (rows_in, rows), (lanes_in, lanes), (twiddle_in, twiddle)])]
    for copy in local:
        copy.start()
    pl.semaphore_wait(barrier, len(senders))

    def remote(src, dst, send_sem, recv_sem, device):
        return pltpu.make_async_remote_copy(src_ref=src, dst_ref=dst, send_sem=send_sem, recv_sem=recv_sem, device_id=device, device_id_type=mesh_id)

    def piece(ref, span):
        return ref.at[:, pl.ds(span[0], span[1])]

    def ring(index, src, slot, part, to):
        span = HALVES[part]
        return remote(piece(src, span), piece(slots.at[slot], span), ring_send.at[index], slot_recv.at[slot, part], (k, to))

    def to_mate(index, src, slot, part):
        span = HALVES[part]
        return remote(piece(src, span), piece(slots.at[slot], span), mate_send.at[index], slot_recv.at[slot, part], (k, mate))

    def take(slot, part):
        ring(0, slots.at[slot], slot, part, band).wait_recv()
    other_down, other_up = (at(1 - y, left, core), at(1 - y, right, core))
    far, other_far = (at(y, across, core), at(1 - y, across, core))
    pool = [remote(occ, occ1, pool_send.at[4], pool_recv.at[4], (ahead, band))]
    pool += [remote(piece(own, span), piece(first, span), pool_send.at[i], pool_recv.at[i], (ahead, band)) for i, span in enumerate(QUARTERS)]
    onward = [remote(occ1, occ2, next_send.at[4], next_recv.at[4], (k, band_up))]
    onward += [remote(piece(first, span), piece(second, span), next_send.at[i], next_recv.at[i], (k, band_up)) for i, span in enumerate(QUARTERS)]
    ring_own = [ring(0, own, band, 0, x_up), ring(1, own, band, 1, x_down), ring(2, own, band, 1, x_up), ring(3, own, band, 0, x_down), ring(4, own, band, 0, y_mate), ring(5, own, band, 1, y_mate)]
    mate_own = [to_mate(0, own, band, 0), to_mate(1, own, band, 1)]
    relays = [(x_down, 0, [ring(6, slots.at[x_down], x_down, 0, x_up)]), (x_up, 1, [ring(7, slots.at[x_up], x_up, 1, x_down)]), (x_down, 1, []), (x_up, 0, []), (y_mate, 0, [ring(8, slots.at[y_mate], y_mate, 0, x_up), ring(9, slots.at[y_mate], y_mate, 0, x_down)]), (y_mate, 1, [ring(10, slots.at[y_mate], y_mate, 1, x_up), ring(11, slots.at[y_mate], y_mate, 1, x_down)]), (far, 0, [ring(12, slots.at[far], far, 0, y_mate)]), (far, 1, [ring(13, slots.at[far], far, 1, y_mate)]), (other_down, 0, []), (other_down, 1, []), (other_up, 0, []), (other_up, 1, []), (other_far, 0, []), (other_far, 1, [])]
    relays = [(slot, part, copies + [to_mate(2 + i, slots.at[slot], slot, part)]) for i, (slot, part, copies) in enumerate(relays)]

    def relay(*which):
        for i in which:
            slot, part, copies = relays[i]
            take(slot, part)
            for copy in copies:
                copy.start()
    twins = [(at(yy, xx, 1 - core), part) for yy in (y, 1 - y) for xx in (x, left, right, across) for part in range(2)]

    def start(copies):
        for copy in copies:
            copy.start()
    early = k == 0

    @pl.when(jnp.logical_not(early))
    def _():
        start(pool)
    start(ring_own[4:])
    start(ring_own[:4])

    @pl.when(early)
    def _():
        start(pool)
    start(mate_own)
    for copy in local:
        copy.wait()
    dense[:, pl.ds(360, 8), :] = jnp.zeros((2, 8, 128), F32)
    for t in range(FULL):
        dense[0, pl.ds(8 * t, 8), :] = flat[pl.ds(BLOCK * t, BLOCK)].reshape(8, 128)
    for j in range(0, TAIL, 128):
        width = min(128, TAIL - j)
        dense[0, 8 * FULL + j // 128, 0:width] = flat[pl.ds(FULL * BLOCK + j, width)]
    to_planes(dense.at[0], planes.at[0])
    permute_scale(planes.at[0], scale)
    unpack(slots.at[band], dense)
    for part in range(2):
        to_planes(dense.at[part], own_planes.at[part])

    @pl.when(early)
    def _():
        relay(*range(8))

    @pl.when(jnp.logical_not(early))
    def _():
        relay(0, 1, 2, 3)
    for arrived, copy in zip(pool, onward):
        arrived.wait_recv()
        copy.start()

    def pair(raw, occupied):
        unpack(raw, dense)
        for part in range(2):
            to_planes(dense.at[part], planes.at[part])
        weight = -0.5 * occupied[...].astype(F32)
        return exchange_pair(own_planes, planes, weight, rows, lanes, twiddle, scale)

    @pl.when(jnp.logical_not(early))
    def _():
        relay(*(4, 5, 6, 7))
    re, im = pair(first, occ1)
    for part, value in enumerate((re, im)):
        accum[part, 0], accum[part, 1] = (value[:, :128], value[:, 128:])

    @pl.when(early)
    def _():
        relay(*range(8, 14))
    for copy in onward:
        copy.wait_recv()
    re, im = pair(second, occ2)
    for part, value in enumerate((re, im)):
        accum[part, 0] += value[:, :128]
        accum[part, 1] += value[:, 128:]

    @pl.when(jnp.logical_not(early))
    def _():
        relay(*range(8, 14))
    for slot, part in twins:
        take(slot, part)
    for copy in pool:
        copy.wait_send()
    for copy in onward + ring_own + mate_own:
        copy.wait_send()
    for _, _, copies in relays:
        for copy in copies:
            copy.wait_send()

def finish_body(accum, slots, out_hbm, gram, out, dense, ket, ket_turned, partial, sem):
    n_band = slots.shape[0]
    for part in range(2):
        to_dense(accum.at[part], dense.at[part])
    partial[...] = jnp.zeros(partial.shape, F32)

    def emit(start_at, width, value):
        span = pl.ds(start_at, width)
        value = value.astype(BF16)
        out[:, span] = value
        ket[:, span] = value.astype(F32)

    def emit_turned(start_at, width, value):
        ket_turned[:, pl.ds(start_at, width)] = value.astype(BF16).astype(F32)
    for t in range(FULL):
        both = dense[:, pl.ds(8 * t, 8), :]
        turned = jnp.concatenate([both[1:2], -both[0:1]], axis=0)
        emit(BLOCK * t, BLOCK, both.reshape(2, BLOCK))
        emit_turned(BLOCK * t, BLOCK, turned.reshape(2, BLOCK))
    for j in range(0, TAIL, 128):
        width = min(128, TAIL - j)
        both = dense[:, 8 * FULL + j // 128, 0:width]
        emit(FULL * BLOCK + j, width, both)
        emit_turned(FULL * BLOCK + j, width, jnp.concatenate([both[1:2], -both[0:1]], axis=0))
    result = pltpu.make_async_copy(out, out_hbm, sem)
    result.start()

    def overlap(step, carry):
        pair = [2 * step, 2 * step + 1]
        totals = [[jnp.zeros((2, BLOCK), F32) for _ in range(WAYS)] for _ in range(4)]
        for t in range(FULL):
            span = pl.ds(BLOCK * t, BLOCK)
            sides = (ket[:, span], ket_turned[:, span])
            for s, slot in enumerate(pair):
                value = slots[slot, :, span].astype(F32)
                for i, side in enumerate(sides):
                    totals[2 * s + i][t % WAYS] += value * side
        for s, slot in enumerate(pair):
            for i, side in enumerate((ket, ket_turned)):
                index = slot + n_band * i
                total = sum(totals[2 * s + i][1:], totals[2 * s + i][0])
                fold = total[:, 0:128]
                for j in range(1, BLOCK // 128):
                    fold += total[:, 128 * j:128 * j + 128]
                for j in range(0, TAIL - 64, 128):
                    span = pl.ds(FULL * BLOCK + j, 128)
                    fold += slots[slot, :, span].astype(F32) * side[:, span]
                span = pl.ds(GRID - 64, 64)
                partial[index, 0:2, :] = fold
                partial[index, 2:4, 0:64] = slots[slot, :, span].astype(F32) * side[:, span]
        return carry
    lax.fori_loop(0, n_band // 2, overlap, 0)
    sums = partial[...].sum(axis=1)
    ones = jnp.full((8, 128), 1.0 / math.sqrt(GRID), F32)
    line = lax.dot_general(ones, sums, (((1,), (1,)), ((), ())), precision=lax.Precision.HIGHEST, preferred_element_type=F32)
    gram[0] = line[0:1, 0:n_band]
    gram[1] = line[0:1, n_band:2 * n_band]
    result.wait()

def pin(value):
    return pltpu.with_memory_space_constraint(value, pltpu.HBM)

def shards(n_pool, orbitals, occupation, kernel):
    n_band = 4 * NX
    vmem = pl.BlockSpec(memory_space=pltpu.VMEM)
    hbm = pl.BlockSpec(memory_space=pltpu.HBM)
    raw = pltpu.VMEM((2, GRID), BF16)
    dma = pltpu.SemaphoreType.DMA
    scalar = pltpu.VMEM((1, 1), jnp.int32)
    plane = pltpu.VMEM((2, 2, SIDE, 128), F32)
    accum, slots = pl.pallas_call(functools.partial(kernel_body, n_pool), out_shape=(jax.ShapeDtypeStruct((2, 2, SIDE, 128), F32), jax.ShapeDtypeStruct((n_band, 2, GRID), BF16)), in_specs=[hbm] * 6, out_specs=(vmem, vmem), scratch_shapes=[raw, raw, scalar, scalar, pltpu.VMEM((GRID,), F32), pltpu.VMEM((2, SIDE, SIDE), BF16), pltpu.VMEM((2, WIDE, WIDE), BF16), pltpu.VMEM((2, SIDE, WIDE), F32), pltpu.VMEM((2, DENSE, 128), F32), plane, plane, pltpu.VMEM((2, SIDE, 128), F32), dma((5,)), dma((5,)), dma((5,)), dma((5,)), dma((5,)), dma((n_band, 2)), dma((14,)), dma((16,))], compiler_params=pltpu.CompilerParams(collective_id=0, has_side_effects=True, vmem_limit_bytes=ROOM), name='exchange')(pin(orbitals.reshape(2, GRID)), occupation, *map(pin, (kernel, *tables())))
    exchanged, gram = pl.pallas_call(finish_body, out_shape=(jax.ShapeDtypeStruct((2, GRID), BF16), jax.ShapeDtypeStruct((2, 1, n_band), F32)), in_specs=[vmem, vmem], out_specs=(hbm, vmem), scratch_shapes=[raw, pltpu.VMEM((2, DENSE, 128), F32), pltpu.VMEM((2, GRID), F32), pltpu.VMEM((2, GRID), F32), pltpu.VMEM((2 * n_band, 8, 128), F32), dma], compiler_params=pltpu.CompilerParams(vmem_limit_bytes=16 * 1024 * 1024), name='finish')(accum, slots)
    return (exchanged.reshape(1, 1, 2, GRID), gram.reshape(1, 2, n_band, 1))

def solution(mesh):
    return jax.shard_map(functools.partial(shards, mesh.shape['pool']), mesh=mesh, in_specs=(P('pool', 'band', None, None), P('pool', 'band'), P()), out_specs=(P('pool', 'band', None, None), P('pool', None, None, 'band')), check_vma=False)
```

```python
import functools
import math
import jax
import jax.numpy as jnp
import numpy as np
from jax import lax
from jax.experimental import pallas as pl
from jax.experimental.pallas import tpu as pltpu
from jax.sharding import PartitionSpec as P
NG = 36
GRID = 46656
SIDE = 216
WIDE = 256
DENSE = 368
BLOCK = 1024
FULL = GRID // BLOCK
TAIL = GRID - FULL * BLOCK
NX = 4
WAYS = 4
ROOM = 50331648
F32 = jnp.float32
BF16 = jnp.bfloat16
HALVES = ((0, 23296), (23296, 23360))
QUARTERS = ((0, 11648), (11648, 11648), (23296, 11648), (34944, 11712))

def tables():
    index = np.arange(SIDE)
    x, y_high = (index // 6, index % 6)
    rows = (np.outer(x, x) + 6 * np.outer(y_high, y_high)) % NG
    y_low, z = (index // NG, index % NG)
    lanes = (np.outer(z, z) + 6 * np.outer(y_low, y_low)) % NG
    twiddle = np.outer(y_high, y_low) % NG
    step = 2.0 * math.pi / NG

    def both(phases, shape):
        out = np.zeros((2,) + shape, np.float32)
        out[:, :SIDE, :SIDE] = np.stack([np.cos(step * phases), np.sin(step * phases)])
        return jnp.asarray(out)
    return (both(rows, (SIDE, SIDE)).astype(BF16), both(lanes, (WIDE, WIDE)).astype(BF16), both(twiddle, (SIDE, WIDE)))

def dot(a, b):
    return jnp.dot(a, b, preferred_element_type=F32)

def lane_index(rows):
    return lax.broadcasted_iota(jnp.int32, (rows, 128), 1)

def unpack(raw, dense):
    for t in range(FULL):
        dense[:, pl.ds(8 * t, 8), :] = raw[:, pl.ds(BLOCK * t, BLOCK)].astype(F32).reshape(2, 8, 128)
    for j in range(0, TAIL, 128):
        width = min(128, TAIL - j)
        dense[:, 8 * FULL + j // 128, 0:width] = raw[:, pl.ds(FULL * BLOCK + j, width)].astype(F32)

def to_planes(dense, planes):
    for start in range(16):
        count = 14 if start < 8 else 13
        row, shift = (SIDE * start // 128, SIDE * start % 128)
        low = dense[pl.ds(row, count, stride=27), :]
        high = dense[pl.ds(row + 1, count, stride=27), :]
        if shift:
            low, high = (pltpu.roll(low, 128 - shift, 1), pltpu.roll(high, 128 - shift, 1))
            keep = lane_index(count) < 128 - shift
            low = jnp.where(keep, low, high)
            if shift + SIDE > 256:
                last = pltpu.roll(dense[pl.ds(row + 2, count, stride=27), :], 128 - shift, 1)
                high = jnp.where(keep, high, last)
        planes[0, pl.ds(start, count, stride=16), :] = low
        planes[1, pl.ds(start, count, stride=16), :] = high

def to_dense(planes, dense):
    for q in range(27):
        count = 14 if q <= 12 else 13
        total, lane = (None, lane_index(count))
        pos = 0
        while pos < 128:
            row, col = divmod(128 * q + pos, SIDE)
            plane, first = (0, 0) if col < 128 else (1, 128)
            width = min((SIDE if plane else 128) - col, 128 - pos)
            piece = planes[plane, pl.ds(row, count, stride=16), :]
            shift = (pos - (col - first)) % 128
            if shift:
                piece = pltpu.roll(piece, shift, 1)
            total = piece if total is None else jnp.where(lane < pos, total, piece)
            pos += width
        dense[pl.ds(q, count, stride=27), :] = total
    row, col = divmod(364 * 128, SIDE)
    dense[364:365, 0:64] = planes[1, row:row + 1, col - 128:col - 64]

def permute_scale(planes, scale):
    lane = lane_index(NG)
    for low in range(6):
        for plane in range(2):
            total = jnp.zeros((NG, 128), F32)
            for high in range(6):
                pos, end = (max(NG * high, 128 * plane), min(NG * high + NG, 128 * plane + 128))
                while pos < end:
                    col = NG * low + pos - NG * high
                    source = col // 128
                    width = min(end - pos, 128 * (source + 1) - col)
                    piece = planes[source, pl.ds(high, NG, stride=6), :]
                    shift = (pos - col) % 128
                    if shift:
                        piece = pltpu.roll(piece, shift, 1)
                    at = pos - 128 * plane
                    total = jnp.where((lane >= at) & (lane < at + width), piece, total)
                    pos += width
            scale[plane, pl.ds(low, NG, stride=6), :] = total * (1.0 / GRID)

def wide(planes):
    return jnp.concatenate([planes[0], planes[1]], axis=1)

def exchange_pair(own, other, weight, rows, lanes, twiddle, scale):
    c, d, a, b = (wide(own.at[0]), wide(own.at[1]), wide(other.at[0]), wide(other.at[1]))
    re, im = ((a * c + b * d).astype(BF16), (a * d - b * c).astype(BF16))
    cos, sin = (rows[0], rows[1])
    turn_re, turn_im = (twiddle[0], twiddle[1])
    u, v = (dot(cos, re) + dot(sin, im), dot(cos, im) - dot(sin, re))
    re, im = ((u * turn_re + v * turn_im).astype(BF16), (v * turn_re - u * turn_im).astype(BF16))
    cos, sin = (lanes[0], lanes[1])
    factor = wide(scale)
    u, v = (dot(re, cos) + dot(im, sin), dot(im, cos) - dot(re, sin))
    re, im = ((u * factor).astype(BF16), (v * factor).astype(BF16))
    u, v = (dot(re, cos) - dot(im, sin), dot(im, cos) + dot(re, sin))
    re, im = ((u * turn_re - v * turn_im).astype(BF16), (v * turn_re + u * turn_im).astype(BF16))
    cos, sin = (rows[0], rows[1])
    e, f = (dot(cos, re) - dot(sin, im), dot(cos, im) + dot(sin, re))
    return (weight * (a * e - b * f), weight * (a * f + b * e))

def kernel_body(n_pool, own, occ, kernel, rows_in, lanes_in, twiddle_in, out, ket, ket_turned, partial, slots, first, second, occ1, occ2, flat, rows, lanes, twiddle, dense, own_planes, planes, accum, scale, local_sem, pool_send, pool_recv, next_send, next_recv, slot_recv, ring_send, mate_send):
    k, band = (lax.axis_index('pool'), lax.axis_index('band'))
    n_band = 4 * NX
    y, x, core = (band // (2 * NX), band // 2 % NX, band % 2)

    def at(yy, xx, cc):
        return yy * (2 * NX) + xx * 2 + cc
    ahead, behind = ((k + 1) % n_pool, (k + n_pool - 1) % n_pool)
    right, left, across = ((x + 1) % NX, (x + NX - 1) % NX, (x + 2) % NX)
    x_up, x_down = (at(y, right, core), at(y, left, core))
    y_mate, mate = (at(1 - y, x, core), at(y, x, 1 - core))
    band_up, band_down = ((band + 1) % n_band, (band + n_band - 1) % n_band)
    mesh_id = pl.DeviceIdType.MESH
    barrier = pltpu.get_barrier_semaphore()
    senders = [(behind, band)] + [(k, b) for b in (band_down, x_up, x_down, y_mate, mate)]
    for device in senders:
        pl.semaphore_signal(barrier, inc=1, device_id=device, device_id_type=mesh_id)
    local = [pltpu.make_async_copy(src, dst, local_sem.at[i]) for i, (src, dst) in enumerate([(own, slots.at[band]), (kernel, flat), (rows_in, rows), (lanes_in, lanes), (twiddle_in, twiddle)])]
    for copy in local:
        copy.start()
    pl.semaphore_wait(barrier, len(senders))

    def remote(src, dst, send_sem, recv_sem, device):
        return pltpu.make_async_remote_copy(src_ref=src, dst_ref=dst, send_sem=send_sem, recv_sem=recv_sem, device_id=device, device_id_type=mesh_id)

    def piece(ref, span):
        return ref.at[:, pl.ds(span[0], span[1])]

    def ring(index, src, slot, part, to):
        span = HALVES[part]
        return remote(piece(src, span), piece(slots.at[slot], span), ring_send.at[index], slot_recv.at[slot, part], (k, to))

    def to_mate(index, src, slot, part):
        span = HALVES[part]
        return remote(piece(src, span), piece(slots.at[slot], span), mate_send.at[index], slot_recv.at[slot, part], (k, mate))

    def take(slot, part):
        ring(0, slots.at[slot], slot, part, band).wait_recv()
    other_down, other_up = (at(1 - y, left, core), at(1 - y, right, core))
    far, other_far = (at(y, across, core), at(1 - y, across, core))
    pool = [remote(occ, occ1, pool_send.at[4], pool_recv.at[4], (ahead, band))]
    pool += [remote(piece(own, span), piece(first, span), pool_send.at[i], pool_recv.at[i], (ahead, band)) for i, span in enumerate(QUARTERS)]
    onward = [remote(occ1, occ2, next_send.at[4], next_recv.at[4], (k, band_up))]
    onward += [remote(piece(first, span), piece(second, span), next_send.at[i], next_recv.at[i], (k, band_up)) for i, span in enumerate(QUARTERS)]
    ring_own = [ring(0, own, band, 0, x_up), ring(1, own, band, 1, x_down), ring(2, own, band, 1, x_up), ring(3, own, band, 0, x_down), ring(4, own, band, 0, y_mate), ring(5, own, band, 1, y_mate)]
    mate_own = [to_mate(0, own, band, 0), to_mate(1, own, band, 1)]
    relays = [(x_down, 0, [ring(6, slots.at[x_down], x_down, 0, x_up)]), (x_up, 1, [ring(7, slots.at[x_up], x_up, 1, x_down)]), (x_down, 1, []), (x_up, 0, []), (y_mate, 0, [ring(8, slots.at[y_mate], y_mate, 0, x_up), ring(9, slots.at[y_mate], y_mate, 0, x_down)]), (y_mate, 1, [ring(10, slots.at[y_mate], y_mate, 1, x_up), ring(11, slots.at[y_mate], y_mate, 1, x_down)]), (far, 0, [ring(12, slots.at[far], far, 0, y_mate)]), (far, 1, [ring(13, slots.at[far], far, 1, y_mate)]), (other_down, 0, []), (other_down, 1, []), (other_up, 0, []), (other_up, 1, []), (other_far, 0, []), (other_far, 1, [])]
    relays = [(slot, part, copies + [to_mate(2 + i, slots.at[slot], slot, part)]) for i, (slot, part, copies) in enumerate(relays)]

    def relay(*which):
        for i in which:
            slot, part, copies = relays[i]
            take(slot, part)
            for copy in copies:
                copy.start()
    twins = [(at(yy, xx, 1 - core), part) for yy in (y, 1 - y) for xx in (x, left, right, across) for part in range(2)]

    def start(copies):
        for copy in copies:
            copy.start()
    early = k == 0

    @pl.when(jnp.logical_not(early))
    def _():
        start(pool)
    start(ring_own[4:])
    start(ring_own[:4])

    @pl.when(early)
    def _():
        start(pool)
    start(mate_own)
    for copy in local:
        copy.wait()
    dense[:, pl.ds(360, 8), :] = jnp.zeros((2, 8, 128), F32)
    for t in range(FULL):
        dense[0, pl.ds(8 * t, 8), :] = flat[pl.ds(BLOCK * t, BLOCK)].reshape(8, 128)
    for j in range(0, TAIL, 128):
        width = min(128, TAIL - j)
        dense[0, 8 * FULL + j // 128, 0:width] = flat[pl.ds(FULL * BLOCK + j, width)]
    to_planes(dense.at[0], planes.at[0])
    permute_scale(planes.at[0], scale)
    unpack(slots.at[band], dense)
    for part in range(2):
        to_planes(dense.at[part], own_planes.at[part])

    @pl.when(early)
    def _():
        relay(*range(8))

    @pl.when(jnp.logical_not(early))
    def _():
        relay(0, 1, 2, 3)
    for arrived, copy in zip(pool, onward):
        arrived.wait_recv()
        copy.start()

    def pair(raw, occupied):
        unpack(raw, dense)
        for part in range(2):
            to_planes(dense.at[part], planes.at[part])
        weight = -0.5 * occupied[...].astype(F32)
        return exchange_pair(own_planes, planes, weight, rows, lanes, twiddle, scale)

    @pl.when(jnp.logical_not(early))
    def _():
        relay(*(4, 5, 6, 7))
    re, im = pair(first, occ1)
    for part, value in enumerate((re, im)):
        accum[part, 0], accum[part, 1] = (value[:, :128], value[:, 128:])

    @pl.when(early)
    def _():
        relay(*range(8, 14))
    for copy in onward:
        copy.wait_recv()
    re, im = pair(second, occ2)
    for part, value in enumerate((re, im)):
        accum[part, 0] += value[:, :128]
        accum[part, 1] += value[:, 128:]

    @pl.when(jnp.logical_not(early))
    def _():
        relay(*range(8, 14))
    emit_result(accum, dense, out, ket, ket_turned)
    partial[...] = jnp.zeros(partial.shape, F32)

    def same(step, carry):
        pair = [4 * step + core, 4 * step + 2 + core]
        overlap(pair, pair, slots, ket, ket_turned, partial)
        return carry
    lax.fori_loop(0, n_band // 4, same, 0)
    for slot, part in twins:
        take(slot, part)
    for copy in pool:
        copy.wait_send()
    for copy in onward + ring_own + mate_own:
        copy.wait_send()
    for _, _, copies in relays:
        for copy in copies:
            copy.wait_send()

def emit_result(accum, dense, out, ket, ket_turned):
    for part in range(2):
        to_dense(accum.at[part], dense.at[part])

    def emit(start_at, width, value, turned):
        span = pl.ds(start_at, width)
        value = value.astype(BF16)
        out[:, span] = value
        ket[:, span] = value.astype(F32)
        ket_turned[:, span] = turned.astype(BF16).astype(F32)
    for t in range(FULL):
        both = dense[:, pl.ds(8 * t, 8), :]
        turned = jnp.concatenate([both[1:2], -both[0:1]], axis=0)
        emit(BLOCK * t, BLOCK, both.reshape(2, BLOCK), turned.reshape(2, BLOCK))
    for j in range(0, TAIL, 128):
        width = min(128, TAIL - j)
        both = dense[:, 8 * FULL + j // 128, 0:width]
        turned = jnp.concatenate([both[1:2], -both[0:1]], axis=0)
        emit(FULL * BLOCK + j, width, both, turned)

def overlap(pair, places, slots, ket, ket_turned, partial):
    totals = [[jnp.zeros((2, BLOCK), F32) for _ in range(WAYS)] for _ in range(4)]
    for t in range(FULL):
        span = pl.ds(BLOCK * t, BLOCK)
        sides = (ket[:, span], ket_turned[:, span])
        for s, slot in enumerate(pair):
            value = slots[slot, :, span].astype(F32)
            for i, side in enumerate(sides):
                totals[2 * s + i][t % WAYS] += value * side
    for s, slot in enumerate(pair):
        for i, side in enumerate((ket, ket_turned)):
            index = places[s] + partial.shape[0] // 2 * i
            total = sum(totals[2 * s + i][1:], totals[2 * s + i][0])
            fold = total[:, 0:128]
            for j in range(1, BLOCK // 128):
                fold += total[:, 128 * j:128 * j + 128]
            for j in range(0, TAIL - 64, 128):
                span = pl.ds(FULL * BLOCK + j, 128)
                fold += slots[slot, :, span].astype(F32) * side[:, span]
            span = pl.ds(GRID - 64, 64)
            partial[index, 0:2, :] = fold
            partial[index, 2:4, 0:64] = slots[slot, :, span].astype(F32) * side[:, span]

def finish_body(out, ket, ket_turned, half, slots, out_hbm, gram, partial, sem):
    n_band = slots.shape[0]
    core = lax.axis_index('band') % 2
    result = pltpu.make_async_copy(out, out_hbm, sem)
    result.start()
    partial[...] = half[...]

    def twin(step, carry):
        pair = [4 * step + 1 - core, 4 * step + 3 - core]
        overlap(pair, pair, slots, ket, ket_turned, partial)
        return carry
    lax.fori_loop(0, n_band // 4, twin, 0)
    sums = partial[...].sum(axis=1)
    ones = jnp.full((8, 128), 1.0 / math.sqrt(GRID), F32)
    line = lax.dot_general(ones, sums, (((1,), (1,)), ((), ())), precision=lax.Precision.HIGHEST, preferred_element_type=F32)
    gram[0] = line[0:1, 0:n_band]
    gram[1] = line[0:1, n_band:2 * n_band]
    result.wait()

def pin(value):
    return pltpu.with_memory_space_constraint(value, pltpu.HBM)

def shards(n_pool, orbitals, occupation, kernel):
    n_band = 4 * NX
    vmem = pl.BlockSpec(memory_space=pltpu.VMEM)
    hbm = pl.BlockSpec(memory_space=pltpu.HBM)
    raw = pltpu.VMEM((2, GRID), BF16)
    dma = pltpu.SemaphoreType.DMA
    scalar = pltpu.VMEM((1, 1), jnp.int32)
    plane = pltpu.VMEM((2, 2, SIDE, 128), F32)
    sums = pltpu.VMEM((2 * n_band, 8, 128), F32)
    results = pl.pallas_call(functools.partial(kernel_body, n_pool), out_shape=(jax.ShapeDtypeStruct((2, GRID), BF16), jax.ShapeDtypeStruct((2, GRID), F32), jax.ShapeDtypeStruct((2, GRID), F32), jax.ShapeDtypeStruct((2 * n_band, 8, 128), F32), jax.ShapeDtypeStruct((n_band, 2, GRID), BF16)), in_specs=[hbm] * 6, out_specs=(vmem,) * 5, scratch_shapes=[raw, raw, scalar, scalar, pltpu.VMEM((GRID,), F32), pltpu.VMEM((2, SIDE, SIDE), BF16), pltpu.VMEM((2, WIDE, WIDE), BF16), pltpu.VMEM((2, SIDE, WIDE), F32), pltpu.VMEM((2, DENSE, 128), F32), plane, plane, plane, pltpu.VMEM((2, SIDE, 128), F32), dma((5,)), dma((5,)), dma((5,)), dma((5,)), dma((5,)), dma((n_band, 2)), dma((14,)), dma((16,))], compiler_params=pltpu.CompilerParams(collective_id=0, has_side_effects=True, vmem_limit_bytes=ROOM), name='exchange')(pin(orbitals.reshape(2, GRID)), occupation, *map(pin, (kernel, *tables())))
    exchanged, gram = pl.pallas_call(finish_body, out_shape=(jax.ShapeDtypeStruct((2, GRID), BF16), jax.ShapeDtypeStruct((2, 1, n_band), F32)), in_specs=[vmem] * 5, out_specs=(hbm, vmem), scratch_shapes=[sums, dma], compiler_params=pltpu.CompilerParams(vmem_limit_bytes=16 * 1024 * 1024), name='finish')(*results)
    return (exchanged.reshape(1, 1, 2, GRID), gram.reshape(1, 2, n_band, 1))

def solution(mesh):
    return jax.shard_map(functools.partial(shards, mesh.shape['pool']), mesh=mesh, in_specs=(P('pool', 'band', None, None), P('pool', 'band'), P()), out_specs=(P('pool', 'band', None, None), P('pool', None, None, 'band')), check_vma=False)
```

```python
import functools
import math
import jax
import jax.numpy as jnp
import numpy as np
from jax import lax
from jax.experimental import pallas as pl
from jax.experimental.pallas import tpu as pltpu
from jax.sharding import PartitionSpec as P
NG = 36
GRID = 46656
SIDE = 216
WIDE = 256
DENSE = 368
BLOCK = 1024
FULL = GRID // BLOCK
TAIL = GRID - FULL * BLOCK
NX = 4
WAYS = 4
ROOM = 50331648
F32 = jnp.float32
BF16 = jnp.bfloat16
HALVES = ((0, 23296), (23296, 23360))
QUARTERS = ((0, 11648), (11648, 11648), (23296, 11648), (34944, 11712))

def tables():
    index = np.arange(SIDE)
    x, y_high = (index // 6, index % 6)
    rows = (np.outer(x, x) + 6 * np.outer(y_high, y_high)) % NG
    y_low, z = (index // NG, index % NG)
    lanes = (np.outer(z, z) + 6 * np.outer(y_low, y_low)) % NG
    twiddle = np.outer(y_high, y_low) % NG
    step = 2.0 * math.pi / NG

    def both(phases, shape):
        out = np.zeros((2,) + shape, np.float32)
        out[:, :SIDE, :SIDE] = np.stack([np.cos(step * phases), np.sin(step * phases)])
        return jnp.asarray(out)
    return (both(rows, (SIDE, SIDE)).astype(BF16), both(lanes, (WIDE, WIDE)).astype(BF16), both(twiddle, (SIDE, WIDE)))

def dot(a, b):
    return jnp.dot(a, b, preferred_element_type=F32)

def lane_index(rows):
    return lax.broadcasted_iota(jnp.int32, (rows, 128), 1)

def unpack(raw, dense):
    for t in range(FULL):
        dense[:, pl.ds(8 * t, 8), :] = raw[:, pl.ds(BLOCK * t, BLOCK)].astype(F32).reshape(2, 8, 128)
    for j in range(0, TAIL, 128):
        width = min(128, TAIL - j)
        dense[:, 8 * FULL + j // 128, 0:width] = raw[:, pl.ds(FULL * BLOCK + j, width)].astype(F32)

def to_planes(dense, planes):
    for start in range(16):
        count = 14 if start < 8 else 13
        row, shift = (SIDE * start // 128, SIDE * start % 128)
        low = dense[pl.ds(row, count, stride=27), :]
        high = dense[pl.ds(row + 1, count, stride=27), :]
        if shift:
            low, high = (pltpu.roll(low, 128 - shift, 1), pltpu.roll(high, 128 - shift, 1))
            keep = lane_index(count) < 128 - shift
            low = jnp.where(keep, low, high)
            if shift + SIDE > 256:
                last = pltpu.roll(dense[pl.ds(row + 2, count, stride=27), :], 128 - shift, 1)
                high = jnp.where(keep, high, last)
        planes[0, pl.ds(start, count, stride=16), :] = low
        planes[1, pl.ds(start, count, stride=16), :] = high

def to_dense(planes, dense):
    for q in range(27):
        count = 14 if q <= 12 else 13
        total, lane = (None, lane_index(count))
        pos = 0
        while pos < 128:
            row, col = divmod(128 * q + pos, SIDE)
            plane, first = (0, 0) if col < 128 else (1, 128)
            width = min((SIDE if plane else 128) - col, 128 - pos)
            piece = planes[plane, pl.ds(row, count, stride=16), :]
            shift = (pos - (col - first)) % 128
            if shift:
                piece = pltpu.roll(piece, shift, 1)
            total = piece if total is None else jnp.where(lane < pos, total, piece)
            pos += width
        dense[pl.ds(q, count, stride=27), :] = total
    row, col = divmod(364 * 128, SIDE)
    dense[364:365, 0:64] = planes[1, row:row + 1, col - 128:col - 64]

def permute_scale(planes, scale):
    lane = lane_index(NG)
    for low in range(6):
        for plane in range(2):
            total = jnp.zeros((NG, 128), F32)
            for high in range(6):
                pos, end = (max(NG * high, 128 * plane), min(NG * high + NG, 128 * plane + 128))
                while pos < end:
                    col = NG * low + pos - NG * high
                    source = col // 128
                    width = min(end - pos, 128 * (source + 1) - col)
                    piece = planes[source, pl.ds(high, NG, stride=6), :]
                    shift = (pos - col) % 128
                    if shift:
                        piece = pltpu.roll(piece, shift, 1)
                    at = pos - 128 * plane
                    total = jnp.where((lane >= at) & (lane < at + width), piece, total)
                    pos += width
            scale[plane, pl.ds(low, NG, stride=6), :] = total * (1.0 / GRID)

def wide(planes):
    return jnp.concatenate([planes[0], planes[1]], axis=1)

def exchange_pair(own, other, weight, rows, lanes, twiddle, scale):
    c, d, a, b = (wide(own.at[0]), wide(own.at[1]), wide(other.at[0]), wide(other.at[1]))
    re, im = ((a * c + b * d).astype(BF16), (a * d - b * c).astype(BF16))
    cos, sin = (rows[0], rows[1])
    turn_re, turn_im = (twiddle[0], twiddle[1])
    u, v = (dot(cos, re) + dot(sin, im), dot(cos, im) - dot(sin, re))
    re, im = ((u * turn_re + v * turn_im).astype(BF16), (v * turn_re - u * turn_im).astype(BF16))
    cos, sin = (lanes[0], lanes[1])
    factor = wide(scale)
    u, v = (dot(re, cos) + dot(im, sin), dot(im, cos) - dot(re, sin))
    re, im = ((u * factor).astype(BF16), (v * factor).astype(BF16))
    u, v = (dot(re, cos) - dot(im, sin), dot(im, cos) + dot(re, sin))
    re, im = ((u * turn_re - v * turn_im).astype(BF16), (v * turn_re + u * turn_im).astype(BF16))
    cos, sin = (rows[0], rows[1])
    e, f = (dot(cos, re) - dot(sin, im), dot(cos, im) + dot(sin, re))
    return (weight * (a * e - b * f), weight * (a * f + b * e))

def kernel_body(n_pool, own, occ, kernel, rows_in, lanes_in, twiddle_in, out, ket, ket_turned, partial, slots, first, second, occ1, occ2, flat, rows, lanes, twiddle, dense, own_planes, planes, accum, scale, local_sem, pool_send, pool_recv, next_send, next_recv, slot_recv, ring_send, mate_send):
    k, band = (lax.axis_index('pool'), lax.axis_index('band'))
    n_band = 4 * NX
    y, x, core = (band // (2 * NX), band // 2 % NX, band % 2)

    def at(yy, xx, cc):
        return yy * (2 * NX) + xx * 2 + cc
    ahead, behind = ((k + 1) % n_pool, (k + n_pool - 1) % n_pool)
    right, left, across = ((x + 1) % NX, (x + NX - 1) % NX, (x + 2) % NX)
    x_up, x_down = (at(y, right, core), at(y, left, core))
    y_mate, mate = (at(1 - y, x, core), at(y, x, 1 - core))
    band_up, band_down = ((band + 1) % n_band, (band + n_band - 1) % n_band)
    mesh_id = pl.DeviceIdType.MESH
    barrier = pltpu.get_barrier_semaphore()
    senders = [(behind, band)] + [(k, b) for b in (band_down, x_up, x_down, y_mate, mate)]
    for device in senders:
        pl.semaphore_signal(barrier, inc=1, device_id=device, device_id_type=mesh_id)
    local = [pltpu.make_async_copy(src, dst, local_sem.at[i]) for i, (src, dst) in enumerate([(own, slots.at[band]), (kernel, flat), (rows_in, rows), (lanes_in, lanes), (twiddle_in, twiddle)])]
    for copy in local:
        copy.start()
    pl.semaphore_wait(barrier, len(senders))

    def remote(src, dst, send_sem, recv_sem, device):
        return pltpu.make_async_remote_copy(src_ref=src, dst_ref=dst, send_sem=send_sem, recv_sem=recv_sem, device_id=device, device_id_type=mesh_id)

    def piece(ref, span):
        return ref.at[:, pl.ds(span[0], span[1])]

    def ring(index, src, slot, part, to):
        span = HALVES[part]
        return remote(piece(src, span), piece(slots.at[slot], span), ring_send.at[index], slot_recv.at[slot, part], (k, to))

    def to_mate(index, src, slot, part):
        span = HALVES[part]
        return remote(piece(src, span), piece(slots.at[slot], span), mate_send.at[index], slot_recv.at[slot, part], (k, mate))

    def take(slot, part):
        ring(0, slots.at[slot], slot, part, band).wait_recv()
    other_down, other_up = (at(1 - y, left, core), at(1 - y, right, core))
    far, other_far = (at(y, across, core), at(1 - y, across, core))
    pool = [remote(occ, occ1, pool_send.at[4], pool_recv.at[4], (ahead, band))]
    pool += [remote(piece(own, span), piece(first, span), pool_send.at[i], pool_recv.at[i], (ahead, band)) for i, span in enumerate(QUARTERS)]
    onward = [remote(occ1, occ2, next_send.at[4], next_recv.at[4], (k, band_up))]
    onward += [remote(piece(first, span), piece(second, span), next_send.at[i], next_recv.at[i], (k, band_up)) for i, span in enumerate(QUARTERS)]
    ring_own = [ring(0, own, band, 0, x_up), ring(1, own, band, 1, x_down), ring(2, own, band, 1, x_up), ring(3, own, band, 0, x_down), ring(4, own, band, 0, y_mate), ring(5, own, band, 1, y_mate)]
    mate_own = [to_mate(0, own, band, 0), to_mate(1, own, band, 1)]
    relays = [(x_down, 0, [ring(6, slots.at[x_down], x_down, 0, x_up)]), (x_up, 1, [ring(7, slots.at[x_up], x_up, 1, x_down)]), (x_down, 1, []), (x_up, 0, []), (y_mate, 0, [ring(8, slots.at[y_mate], y_mate, 0, x_up), ring(9, slots.at[y_mate], y_mate, 0, x_down)]), (y_mate, 1, [ring(10, slots.at[y_mate], y_mate, 1, x_up), ring(11, slots.at[y_mate], y_mate, 1, x_down)]), (far, 0, [ring(12, slots.at[far], far, 0, y_mate)]), (far, 1, [ring(13, slots.at[far], far, 1, y_mate)]), (other_down, 0, []), (other_down, 1, []), (other_up, 0, []), (other_up, 1, []), (other_far, 0, []), (other_far, 1, [])]
    relays = [(slot, part, copies + [to_mate(2 + i, slots.at[slot], slot, part)]) for i, (slot, part, copies) in enumerate(relays)]

    def relay(*which):
        for i in which:
            slot, part, copies = relays[i]
            take(slot, part)
            for copy in copies:
                copy.start()
    twins = [(at(yy, xx, 1 - core), part) for yy in (y, 1 - y) for xx in (x, left, right, across) for part in range(2)]

    def start(copies):
        for copy in copies:
            copy.start()
    early = k == 0
    held = k == n_pool - 2
    final = k == n_pool - 1

    @pl.when(jnp.logical_not(early | held))
    def _():
        start(pool)
    start(ring_own[4:])
    start(ring_own[:4])

    @pl.when(early)
    def _():
        start(pool)
    start(mate_own)
    for copy in local:
        copy.wait()
    dense[:, pl.ds(360, 8), :] = jnp.zeros((2, 8, 128), F32)
    for t in range(FULL):
        dense[0, pl.ds(8 * t, 8), :] = flat[pl.ds(BLOCK * t, BLOCK)].reshape(8, 128)
    for j in range(0, TAIL, 128):
        width = min(128, TAIL - j)
        dense[0, 8 * FULL + j // 128, 0:width] = flat[pl.ds(FULL * BLOCK + j, width)]
    to_planes(dense.at[0], planes.at[0])
    permute_scale(planes.at[0], scale)
    unpack(slots.at[band], dense)
    for part in range(2):
        to_planes(dense.at[part], own_planes.at[part])

    @pl.when(held)
    def _():
        start(pool)

    @pl.when(early)
    def _():
        relay(*range(8))

    @pl.when(jnp.logical_not(early))
    def _():
        relay(0, 1, 2, 3)
    for arrived, copy in zip(pool, onward):
        arrived.wait_recv()
        copy.start()

    def pair(raw, occupied):
        unpack(raw, dense)
        for part in range(2):
            to_planes(dense.at[part], planes.at[part])
        weight = -0.5 * occupied[...].astype(F32)
        return exchange_pair(own_planes, planes, weight, rows, lanes, twiddle, scale)

    @pl.when(jnp.logical_not(early))
    def _():
        relay(*(4, 5, 6, 7))
    re, im = pair(first, occ1)
    for part, value in enumerate((re, im)):
        accum[part, 0], accum[part, 1] = (value[:, :128], value[:, 128:])

    @pl.when(early)
    def _():
        relay(*range(8, 14))
    for copy in onward:
        copy.wait_recv()
    re, im = pair(second, occ2)
    for part, value in enumerate((re, im)):
        accum[part, 0] += value[:, :128]
        accum[part, 1] += value[:, 128:]

    @pl.when(jnp.logical_not(early))
    def _():
        relay(*range(8, 14))
    emit_result(accum, dense, out, ket, ket_turned)
    partial[...] = jnp.zeros(partial.shape, F32)

    def same(step, carry):
        pair = [4 * step + core, 4 * step + 2 + core]
        overlap(pair, pair, slots, ket, ket_turned, partial)
        return carry
    lax.fori_loop(0, n_band // 4, same, 0)
    for slot, part in twins:
        take(slot, part)
    for copy in pool:
        copy.wait_send()
    for copy in onward + ring_own + mate_own:
        copy.wait_send()
    for _, _, copies in relays:
        for copy in copies:
            copy.wait_send()

def emit_result(accum, dense, out, ket, ket_turned):
    for part in range(2):
        to_dense(accum.at[part], dense.at[part])

    def emit(start_at, width, value, turned):
        span = pl.ds(start_at, width)
        value = value.astype(BF16)
        out[:, span] = value
        ket[:, span] = value.astype(F32)
        ket_turned[:, span] = turned.astype(BF16).astype(F32)
    for t in range(FULL):
        both = dense[:, pl.ds(8 * t, 8), :]
        turned = jnp.concatenate([both[1:2], -both[0:1]], axis=0)
        emit(BLOCK * t, BLOCK, both.reshape(2, BLOCK), turned.reshape(2, BLOCK))
    for j in range(0, TAIL, 128):
        width = min(128, TAIL - j)
        both = dense[:, 8 * FULL + j // 128, 0:width]
        turned = jnp.concatenate([both[1:2], -both[0:1]], axis=0)
        emit(FULL * BLOCK + j, width, both, turned)

def overlap(pair, places, slots, ket, ket_turned, partial):
    totals = [[jnp.zeros((2, BLOCK), F32) for _ in range(WAYS)] for _ in range(4)]
    for t in range(FULL):
        span = pl.ds(BLOCK * t, BLOCK)
        sides = (ket[:, span], ket_turned[:, span])
        for s, slot in enumerate(pair):
            value = slots[slot, :, span].astype(F32)
            for i, side in enumerate(sides):
                totals[2 * s + i][t % WAYS] += value * side
    for s, slot in enumerate(pair):
        for i, side in enumerate((ket, ket_turned)):
            index = places[s] + partial.shape[0] // 2 * i
            total = sum(totals[2 * s + i][1:], totals[2 * s + i][0])
            fold = total[:, 0:128]
            for j in range(1, BLOCK // 128):
                fold += total[:, 128 * j:128 * j + 128]
            for j in range(0, TAIL - 64, 128):
                span = pl.ds(FULL * BLOCK + j, 128)
                fold += slots[slot, :, span].astype(F32) * side[:, span]
            span = pl.ds(GRID - 64, 64)
            partial[index, 0:2, :] = fold
            partial[index, 2:4, 0:64] = slots[slot, :, span].astype(F32) * side[:, span]

def finish_body(out, ket, ket_turned, half, slots, out_hbm, gram, partial, sem):
    n_band = slots.shape[0]
    core = lax.axis_index('band') % 2
    result = pltpu.make_async_copy(out, out_hbm, sem)
    result.start()
    partial[...] = half[...]

    def twin(step, carry):
        pair = [4 * step + 1 - core, 4 * step + 3 - core]
        overlap(pair, pair, slots, ket, ket_turned, partial)
        return carry
    lax.fori_loop(0, n_band // 4, twin, 0)
    sums = partial[...].sum(axis=1)
    ones = jnp.full((8, 128), 1.0 / math.sqrt(GRID), F32)
    line = lax.dot_general(ones, sums, (((1,), (1,)), ((), ())), precision=lax.Precision.HIGHEST, preferred_element_type=F32)
    gram[0] = line[0:1, 0:n_band]
    gram[1] = line[0:1, n_band:2 * n_band]
    result.wait()

def pin(value):
    return pltpu.with_memory_space_constraint(value, pltpu.HBM)

def shards(n_pool, orbitals, occupation, kernel):
    n_band = 4 * NX
    vmem = pl.BlockSpec(memory_space=pltpu.VMEM)
    hbm = pl.BlockSpec(memory_space=pltpu.HBM)
    raw = pltpu.VMEM((2, GRID), BF16)
    dma = pltpu.SemaphoreType.DMA
    scalar = pltpu.VMEM((1, 1), jnp.int32)
    plane = pltpu.VMEM((2, 2, SIDE, 128), F32)
    sums = pltpu.VMEM((2 * n_band, 8, 128), F32)
    results = pl.pallas_call(functools.partial(kernel_body, n_pool), out_shape=(jax.ShapeDtypeStruct((2, GRID), BF16), jax.ShapeDtypeStruct((2, GRID), F32), jax.ShapeDtypeStruct((2, GRID), F32), jax.ShapeDtypeStruct((2 * n_band, 8, 128), F32), jax.ShapeDtypeStruct((n_band, 2, GRID), BF16)), in_specs=[hbm] * 6, out_specs=(vmem,) * 5, scratch_shapes=[raw, raw, scalar, scalar, pltpu.VMEM((GRID,), F32), pltpu.VMEM((2, SIDE, SIDE), BF16), pltpu.VMEM((2, WIDE, WIDE), BF16), pltpu.VMEM((2, SIDE, WIDE), F32), pltpu.VMEM((2, DENSE, 128), F32), plane, plane, plane, pltpu.VMEM((2, SIDE, 128), F32), dma((5,)), dma((5,)), dma((5,)), dma((5,)), dma((5,)), dma((n_band, 2)), dma((14,)), dma((16,))], compiler_params=pltpu.CompilerParams(collective_id=0, has_side_effects=True, vmem_limit_bytes=ROOM), name='exchange')(pin(orbitals.reshape(2, GRID)), occupation, *map(pin, (kernel, *tables())))
    exchanged, gram = pl.pallas_call(finish_body, out_shape=(jax.ShapeDtypeStruct((2, GRID), BF16), jax.ShapeDtypeStruct((2, 1, n_band), F32)), in_specs=[vmem] * 5, out_specs=(hbm, vmem), scratch_shapes=[sums, dma], compiler_params=pltpu.CompilerParams(vmem_limit_bytes=16 * 1024 * 1024), name='finish')(*results)
    return (exchanged.reshape(1, 1, 2, GRID), gram.reshape(1, 2, n_band, 1))

def solution(mesh):
    return jax.shard_map(functools.partial(shards, mesh.shape['pool']), mesh=mesh, in_specs=(P('pool', 'band', None, None), P('pool', 'band'), P()), out_specs=(P('pool', 'band', None, None), P('pool', None, None, 'band')), check_vma=False)
```
